32 devices in a mesh: parts: 2 (over y), seq: 16 (over z, x, core).
Axes of the slice: x: 2, y: 2, z: 4, core: 2. Of those that a mesh axis runs over, the one named last changes fastest.
Arguments:
- ids: int32 [8192], P(('parts', 'seq')), parts along dimension 0, may hold values from 0 to 15
- exponents: int32 [16, 8192], P(None, ('parts', 'seq')), parts along dimension 1, may hold values from 1 to 8192
- embedding: bfloat16 [16, 1024], replicated, may hold values from -6 to 6
- norm_gain: float32 [1024], replicated, may hold values from 0.5 to 1.5
- in_proj: bfloat16 [1024, 2304], replicated, may hold values from -0.1875 to 0.1875
- conv_weight: float32 [2, 4, 1280], replicated, may hold values from -3 to 3
- conv_bias: float32 [2, 1280], replicated, may hold values from -3 to 3
- rates: float32 [2, 16], replicated, may hold values from 2.4414063e-05 to 0.016666667
- head_gain: float32 [2, 1024], replicated, may hold values from 0.25 to 1.75
- out_proj: bfloat16 [1024, 1024], replicated, may hold values from -0.125 to 0.125
Outputs:
- mixed: bfloat16 [8192, 1024], P(('parts', 'seq')), parts along dimension 0
The draws below stay inside these ranges and needn't reach their ends.
There are 2 independent parts, one for each index of `parts`. The reference program is written for one: setup_inputs(seed, part) draws one part's arguments, and reference() takes and returns one part's arrays. A program takes and returns all parts, laid end to end along the dimension named above; an argument that names none is the same for every part. Nothing has to cross between parts.
All inputs are finite; a program needn't handle non-finite values.
Results may differ from the reference program's by a relative error of at most 0.0071.
Values may be sent and summed in bfloat16 or wider, within the bound.
No kernel may reach another device: no remote copies, remote signals or barrier semaphores. Data moves between devices by JAX's collectives and lax.ppermute only.
A program may use at most 384 MiB of HBM per device.

```python
import jax
import jax.numpy as jnp
from jax import lax

D = 1024
HEADS = 16
HEAD_DIM = 64
STATE = 128
VOCAB = 16
SPAN = 256
CONV = 4
SURGE_SITE_COUNT = 3
TOK_DEV = 256
INNER = 1024
WIDE = 1280
GENOME_EXTENT = 4096


def draw_exponents(key, part):
    level_key, base_key, placing_seed = jax.random.split(key, 3)
    block_count = GENOME_EXTENT // TOK_DEV
    level_draw = 1 + 4 * jax.random.randint(level_key, (block_count,), 0, 2)
    width_row = jnp.repeat(level_draw, TOK_DEV, total_repeat_length=GENOME_EXTENT)
    base_draw = jax.random.randint(base_key, (HEADS, GENOME_EXTENT), 0, 1 << 20)
    fading_power = 1 + base_draw % width_row[None, :]
    surge_indices = jax.random.randint(placing_seed, (SURGE_SITE_COUNT,), 0, GENOME_EXTENT)
    surge_indicator = jnp.sum((jnp.arange(GENOME_EXTENT)[:, None] == surge_indices[None, :]).astype(jnp.int32), axis=1) > 0
    return jnp.where(surge_indicator[None, :], 2 * GENOME_EXTENT, fading_power).astype(jnp.int32)


def draw_rates(key, part):
    pick_key, slow_key, fast_key = jax.random.split(key, 3)
    fast_share = 0.5
    pick_draw = jax.random.uniform(pick_key, (2, HEADS), jnp.float32)
    slow_rate = jnp.exp(jax.random.uniform(slow_key, (2, HEADS), jnp.float32, jnp.log(0.2), jnp.log(0.4))) / (2.0 * GENOME_EXTENT)
    fast_rate = jnp.exp(jax.random.uniform(fast_key, (2, HEADS), jnp.float32, jnp.log(1.0 / 50.0), jnp.log(1.0 / 30.0))) / 2.0
    return jnp.where(pick_draw < fast_share, fast_rate, slow_rate).astype(jnp.float32)


def plant(values, rng, low, largest):
    spot = [jax.random.randint(jax.random.fold_in(rng, axis), (), 0, length) for axis, length in enumerate(values.shape)]
    longest = values.shape.index(max(values.shape))
    next_to = spot[:longest] + [(spot[longest] + 1) % values.shape[longest]] + spot[longest + 1:]
    return values.at[tuple(spot)].set(low).at[tuple(next_to)].set(largest)


def centred(rng, shape, scale, limit, held_as=jnp.bfloat16):
    return jnp.clip(scale * jax.random.normal(rng, shape, jnp.float32), -limit, limit).astype(held_as)


def setup_inputs(seed: int = 0, part: int = 0) -> dict:
    arg_keys = jax.random.split(jax.random.key(seed), 11)
    own_keys = jax.random.split(jax.random.fold_in(arg_keys[10], part), 11)
    return {
        "ids": plant(jax.random.randint(own_keys[0], (GENOME_EXTENT,), 0, VOCAB), jax.random.fold_in(own_keys[0], 1), 0, VOCAB - 1).astype(jnp.int32),
        "exponents": draw_exponents(jax.random.fold_in(jax.random.fold_in(arg_keys[10], part), 71), part),
        "embedding": centred(arg_keys[2], (VOCAB, D), 1.0, 6.0),
        "norm_gain": jnp.clip(1.0 + 0.1 * jax.random.normal(arg_keys[3], (D,), jnp.float32), 0.5, 1.5),
        "in_proj": centred(arg_keys[4], (D, INNER + WIDE), D ** -0.5, 0.1875),
        "conv_weight": centred(arg_keys[5], (2, CONV, WIDE), 0.5, 3.0, jnp.float32),
        "conv_bias": centred(arg_keys[6], (2, WIDE), 0.5, 3.0, jnp.float32),
        "rates": draw_rates(jax.random.fold_in(arg_keys[10], 71), part),
        "head_gain": jnp.clip(1.0 + 0.15 * jax.random.normal(arg_keys[8], (2, INNER), jnp.float32), 0.25, 1.75),
        "out_proj": centred(arg_keys[9], (INNER, D), (2 * INNER) ** -0.5, 0.125),
    }


eps = 1e-05

def conv_causal(conv_input, tap_weights, bias_row):
    tap_count = tap_weights.shape[0]
    length = conv_input.shape[0]
    padded = jnp.concatenate([jnp.zeros((tap_count - 1, conv_input.shape[1]), conv_input.dtype), conv_input], axis=0)
    running = jnp.zeros(conv_input.shape, jnp.float32) + bias_row[None, :]
    for offset in range(tap_count):
        running = running + tap_weights[offset][None, :] * padded[offset:offset + length].astype(jnp.float32)
    return jax.nn.silu(running).astype(jnp.bfloat16)

def branch(convolved_output, log_decay):
    length = convolved_output.shape[0]
    block_count = length // SPAN
    x_heads = convolved_output[:, :INNER].reshape(block_count, SPAN, HEADS, HEAD_DIM)
    b_rows = convolved_output[:, INNER:INNER + STATE].reshape(block_count, SPAN, STATE)
    c_rows = convolved_output[:, INNER + STATE:].reshape(block_count, SPAN, STATE)
    l_rows = jnp.transpose(log_decay.reshape(HEADS, block_count, SPAN), (1, 0, 2))
    causal = jnp.arange(SPAN)[:, None] >= jnp.arange(SPAN)[None, :]

    def span_step(carry_in, inputs):
        input_span, b_span, c_span, l_span = inputs
        cumulative = jnp.cumsum(l_span, axis=1)
        scores = jnp.dot(c_span, b_span.T, preferred_element_type=jnp.float32)
        log_gap = jnp.where(causal[None], cumulative[:, :, None] - cumulative[:, None, :], -jnp.inf)
        weights = (scores[None] * jnp.exp(log_gap)).astype(jnp.bfloat16)
        y_diag = jnp.einsum('hij,jhp->ihp', weights.astype(jnp.float32), input_span.astype(jnp.float32))
        carried = jnp.einsum('hpn,in->ihp', carry_in, c_span.astype(jnp.float32), precision=lax.Precision.HIGHEST)
        outputs = y_diag + jnp.exp(cumulative).T[:, :, None] * carried
        tail_decay = jnp.exp(cumulative[:, -1:] - cumulative)
        x_scaled = (input_span.astype(jnp.float32) * tail_decay.T[:, :, None]).astype(jnp.bfloat16)
        states = jnp.einsum('jhp,jn->hpn', x_scaled.astype(jnp.float32), b_span.astype(jnp.float32))
        new_state = jnp.exp(cumulative[:, -1])[:, None, None] * carry_in + states
        return (new_state, outputs)
    zero_state = jnp.zeros((HEADS, HEAD_DIM, STATE), jnp.float32)
    _, outputs = lax.scan(span_step, zero_state, (x_heads, b_rows, c_rows, l_rows))
    return outputs.reshape(length, INNER)

def gated_norm(ssm_out, gate_rows, gain_row):
    v_rows = ssm_out * jax.nn.silu(gate_rows.astype(jnp.float32))
    grouped = v_rows.reshape(v_rows.shape[0], HEADS, HEAD_DIM)
    inv_scale = lax.rsqrt(lax.optimization_barrier(jnp.mean(grouped * grouped, axis=2, keepdims=True)) + eps)
    return ((grouped * inv_scale).reshape(v_rows.shape[0], INNER) * gain_row[None, :]).astype(jnp.bfloat16)

def reference(ids, exponents, embedding, norm_gain, in_proj, conv_weight, conv_bias, rates, head_gain, out_proj):
    embed32 = embedding.astype(jnp.float32)
    norm_table = (embed32 * lax.rsqrt(lax.optimization_barrier(jnp.mean(embed32 * embed32, axis=1, keepdims=True)) + eps) * norm_gain[None, :]).astype(jnp.bfloat16)
    projected = jnp.dot(norm_table, in_proj, preferred_element_type=jnp.float32).astype(jnp.bfloat16)
    token_rows = jnp.take(projected, ids, axis=0)
    gate_input = token_rows[:, :INNER]
    conv_input = token_rows[:, INNER:]
    expo_float = exponents.astype(jnp.float32)
    conv_fwd = conv_causal(conv_input, conv_weight[0], conv_bias[0])
    ssm_fwd = branch(conv_fwd, -rates[0][:, None] * expo_float)
    branch_fwd = gated_norm(ssm_fwd, gate_input, head_gain[0])
    conv_rev = conv_causal(jnp.flip(conv_input, 0), conv_weight[1], conv_bias[1])
    ssm_rev = branch(conv_rev, -rates[1][:, None] * jnp.flip(expo_float, 1))
    branch_rev = jnp.flip(gated_norm(ssm_rev, jnp.flip(gate_input, 0), head_gain[1]), 0)
    mixed = jnp.dot(branch_fwd, out_proj, preferred_element_type=jnp.float32) + jnp.dot(branch_rev, out_proj, preferred_element_type=jnp.float32)
    return mixed.astype(jnp.bfloat16)
```

```python
import functools

import jax
import jax.numpy as jnp
from jax import lax
from jax.experimental import pallas as pl
from jax.experimental.pallas import tpu as pltpu
from jax.sharding import PartitionSpec as P

EPS = 1e-05
LOG2E = 1.4426950408889634
F32 = jnp.float32
BF16 = jnp.bfloat16
NT = (((1,), (1,)), ((), ()))
TN = (((0,), (0,)), ((), ()))
VMEM_LIMIT = 56 * 1024 * 1024


def dot(a, b, dims=(((1,), (0,)), ((), ()))):
    return lax.dot_general(a, b, dims, preferred_element_type=F32)


def split(value):
    high = value.astype(BF16)
    return high, (value - high.astype(F32)).astype(BF16)


def tables_kernel(emb_ref, gain_ref, in_ref, cw_ref, cb_ref, hg_ref, conv_ref, gate_ref, hgt_ref):
    vocab = emb_ref.shape[0]
    inner = hg_ref.shape[1]
    wide = cw_ref.shape[2]
    taps = cw_ref.shape[1]
    e = emb_ref[...].astype(F32)
    norm = e * lax.rsqrt(jnp.mean(e * e, axis=1, keepdims=True) + EPS) * gain_ref[...]
    norm = norm.astype(BF16)
    gate = dot(norm, in_ref[:, :inner]).astype(BF16).astype(F32)
    gate = gate / (1.0 + jnp.exp(-gate))
    g0 = gate.astype(BF16)
    g1, g2 = split(gate - g0.astype(F32))
    pad = jnp.zeros((gate_ref.shape[1] - 3 * vocab, inner), BF16)
    gate_ref[...] = jnp.concatenate([g0, g1, g2, pad], axis=0).T
    proj = dot(norm, in_ref[:, inner:]).astype(BF16).astype(F32)
    for b in range(2):
        rows = []
        for j in range(taps):
            row = cw_ref[b, j : j + 1, :] * proj
            if j == taps - 1:
                row = row + cb_ref[b : b + 1, :]
            rows.append(0.5 * row)
        high, low = split(jnp.concatenate(rows, axis=0))
        conv_ref[b] = jnp.concatenate([high, low], axis=0).T
    hg = jnp.concatenate([hg_ref[...], jnp.zeros((126, inner), F32)], axis=0)
    hgt_ref[...] = hg.T


def mixer_kernel(
    count, bits,
    me_ref, rates_ref, data_ref, conv_ref, gate_ref, hgt_ref, out_proj_ref,
    mixed_ref,
    expo, within, total, ids, shifted, state, mixin,
):
    heads, span = data_ref.shape[1], data_ref.shape[2]
    inner = out_proj_ref.shape[0]
    head = inner // heads
    wide = conv_ref.shape[1]
    width = (wide - inner) // 2
    vocab = conv_ref.shape[2] // 8
    me = me_ref[0]

    def unpack(c, _):
        away = jnp.bitwise_xor(me, c)
        slot = jnp.int32(0)
        for i in range(bits):
            slot = slot + (((away >> i) & 1) << (bits - 1 - i))
        raw = data_ref[slot]
        expo[c] = (raw & 0xFFFF) + 1
        ids[pl.ds(c, 1), :] = raw[0:1] >> 16
        return 0

    for c in range(count) if count <= 32 else ():
        unpack(c, 0)
    if count > 32:
        lax.fori_loop(0, count, unpack, 0)

    e = expo[...].reshape(count * heads, span)
    lower = lax.broadcasted_iota(jnp.int32, (span, span), 0)
    upper = lax.broadcasted_iota(jnp.int32, (span, span), 1)
    before = jnp.where(lower < upper, 1.0, 0.0).astype(BF16)
    pre = 256.0 * dot((e >> 8).astype(F32).astype(BF16), before) + dot(
        (e & 255).astype(F32).astype(BF16), before
    )
    within[0] = pre.reshape(count, heads, span)
    inc = pre + e.astype(F32)
    tot = jnp.broadcast_to(inc[:, span - 1 :], inc.shape)
    total[...] = tot.reshape(count, heads, span)
    within[1] = (tot - inc).reshape(count, heads, span)

    tok = ids[...]
    lane = lax.broadcasted_iota(jnp.int32, tok.shape, 1)
    row = lax.broadcasted_iota(jnp.int32, tok.shape, 0)
    for d in range(-3, 4):
        if d == 0:
            moved = tok
        elif d < 0:
            here = pltpu.roll(tok, -d, axis=1)
            other = jnp.where(row == 0, -1, pltpu.roll(here, 1, axis=0))
            moved = jnp.where(lane < -d, other, here)
        else:
            here = pltpu.roll(tok, span - d, axis=1)
            other = jnp.where(row == count - 1, -1, pltpu.roll(here, count - 1, axis=0))
            moved = jnp.where(lane >= span - d, other, here)
        shifted[d + 3] = moved

    values = lax.broadcasted_iota(jnp.int32, (vocab, span), 0)

    def onehot(c, sign):
        rows = []
        for j in range(4):
            token = shifted[3 + (j - 3) * sign, pl.ds(c, 1), :]
            rows.append(jnp.where(values == token, 1.0, 0.0))
        one = jnp.concatenate(rows, axis=0).astype(BF16)
        return jnp.concatenate([one, one], axis=0)

    def convolve(table, one):
        half = dot(table, one)
        return half + half * jnp.tanh(half)

    def rate_of(b, value):
        col = [rates_ref[b, h] * value[h : h + 1] for h in range(heads)]
        return jnp.concatenate(col, axis=0)

    state[...] = jnp.zeros_like(state)

    def remote(i, run):
        rev = i >= me
        b = rev.astype(jnp.int32)
        c = jnp.where(rev, i + 1, me - 1 - i)
        run = jnp.where(i == me, 0.0, run)
        dist = within[1 - b, c] + run
        decay = jnp.exp(-rate_of(b, dist))
        one = onehot(c, 1 - 2 * b)
        x = convolve(conv_ref[b, :inner, :], one)
        x = x.reshape(heads, head, span) * decay[:, None, :]
        x = x.reshape(inner, span).astype(BF16)
        bt = convolve(conv_ref[b, inner : inner + width, :], one).astype(BF16)
        state[b] += dot(x, bt, NT)
        return run + total[c]

    lax.fori_loop(0, count - 1, remote, jnp.zeros((heads, span), F32))

    own_pre = within[0, me]
    own_inc = own_pre + expo[me].astype(F32)
    own_tot = total[me]
    current = jnp.where(values == ids[pl.ds(me, 1), :], 1.0, 0.0).astype(BF16)
    current = jnp.concatenate(
        [current] * 3 + [jnp.zeros((gate_ref.shape[1] - 3 * vocab, span), BF16)], axis=0
    )
    gates = dot(gate_ref[...], current)
    for b in range(2):
        one = onehot(me, 1 - 2 * b)
        conv = convolve(conv_ref[b], one).astype(BF16)
        xt = conv[:inner]
        bt = conv[inner : inner + width]
        ct = conv[inner + width :]
        scores = dot(bt, ct, TN)
        cum = own_inc if b == 0 else own_pre
        cum_col = cum.T
        reach = own_inc if b == 0 else own_tot - own_pre
        high, low = split(state[b])
        carried = dot(
            jnp.concatenate([high, low], axis=1), jnp.concatenate([ct, ct], axis=0)
        )
        keep = lower <= upper if b == 0 else lower >= upper
        for h in range(heads):
            rows = slice(h * head, (h + 1) * head)
            rate = rates_ref[b, h]
            gap = cum[h : h + 1] - cum_col[:, h : h + 1]
            factor = -LOG2E if b == 0 else LOG2E
            w = jnp.where(keep, scores * jnp.exp2(gap * (rate * factor)), 0.0).astype(BF16)
            y = dot(xt[rows], w)
            y = y + jnp.exp(-rate * reach[h : h + 1]) * carried[rows]
            v = y * gates[rows]
            inv = lax.rsqrt(jnp.sum(v * v, axis=0, keepdims=True) * (1.0 / head) + EPS)
            out = v * inv * hgt_ref[rows, b : b + 1]
            if b == 0:
                mixin[rows] = out
            else:
                mixin[rows] = mixin[rows] + out
    mixed_ref[...] = dot(mixin[...].astype(BF16), out_proj_ref[...], TN).astype(BF16)


def shards(
    ids, exponents, embedding, norm_gain, in_proj, conv_weight, conv_bias, rates, head_gain, out_proj
):
    count = lax.axis_size("seq")
    me = lax.axis_index("seq")
    bits = count.bit_length() - 1
    heads, span = exponents.shape
    vocab = embedding.shape[0]
    inner = out_proj.shape[0]
    wide = conv_bias.shape[1]
    width = (wide - inner) // 2
    taps = conv_weight.shape[1]
    params = pltpu.CompilerParams(vmem_limit_bytes=VMEM_LIMIT)
    vmem = pl.BlockSpec(memory_space=pltpu.VMEM)
    smem = pl.BlockSpec(memory_space=pltpu.SMEM)

    conv_table, gate_table, gain_table = pl.pallas_call(
        tables_kernel,
        out_shape=(
            jax.ShapeDtypeStruct((2, wide, 2 * taps * vocab), BF16),
            jax.ShapeDtypeStruct((inner, 128), BF16),
            jax.ShapeDtypeStruct((inner, 128), F32),
        ),
        in_specs=[vmem] * 6,
        out_specs=(vmem, vmem, vmem),
        compiler_params=params,
        name="tables",
        cost_estimate=pl.CostEstimate(flops=80_000_000, bytes_accessed=6_000_000, transcendentals=16384),
    )(embedding, norm_gain[None, :], in_proj, conv_weight, conv_bias, head_gain)

    held = ((exponents - 1) + (ids << 16)[None, :])[None]
    for bit in reversed(range(bits)):
        far = 1 << bit
        other = lax.ppermute(held, "seq", [(i, i ^ far) for i in range(count)])
        held = jnp.concatenate([held, other], axis=0)

    return pl.pallas_call(
        functools.partial(mixer_kernel, count, bits),
        out_shape=jax.ShapeDtypeStruct((span, inner), BF16),
        in_specs=[smem, smem] + [vmem] * 5,
        out_specs=vmem,
        scratch_shapes=[
            pltpu.VMEM((count, heads, span), jnp.int32),
            pltpu.VMEM((2, count, heads, span), F32),
            pltpu.VMEM((count, heads, span), F32),
            pltpu.VMEM((count, span), jnp.int32),
            pltpu.VMEM((7, count, span), jnp.int32),
            pltpu.VMEM((2, inner, width), F32),
            pltpu.VMEM((inner, span), F32),
        ],
        compiler_params=params,
        name="mixer",
        cost_estimate=pl.CostEstimate(flops=12_000_000_000, bytes_accessed=6_000_000, transcendentals=8_000_000),
    )(me[None].astype(jnp.int32), rates, held, conv_table, gate_table, gain_table, out_proj)


def solution(mesh):
    in_specs = (
        P(("parts", "seq")),
        P(None, ("parts", "seq")),
        P(), P(), P(), P(), P(), P(), P(), P(),
    )
    out_specs = P(("parts", "seq"), None)
    return jax.shard_map(shards, mesh=mesh, in_specs=in_specs, out_specs=out_specs, check_vma=False)
```

```python
import functools

import jax
import jax.numpy as jnp
from jax import lax
from jax.experimental import pallas as pl
from jax.experimental.pallas import tpu as pltpu
from jax.sharding import PartitionSpec as P

EPS = 1e-05
LOG2E = 1.4426950408889634
F32 = jnp.float32
BF16 = jnp.bfloat16
NT = (((1,), (1,)), ((), ()))
TN = (((0,), (0,)), ((), ()))
MIB = 1024 * 1024
LANES = 128


def dot(a, b, dims=(((1,), (0,)), ((), ()))):
    return lax.dot_general(a, b, dims, preferred_element_type=F32)


def split(value):
    high = value.astype(BF16)
    return high, (value - high.astype(F32)).astype(BF16)


def sums_before(e):
    span = e.shape[1]
    lower = lax.broadcasted_iota(jnp.int32, (span, span), 0)
    upper = lax.broadcasted_iota(jnp.int32, (span, span), 1)
    before = jnp.where(lower < upper, 1.0, 0.0).astype(BF16)
    high = dot((e >> 8).astype(F32).astype(BF16), before)
    low = dot((e & 255).astype(F32).astype(BF16), before)
    return 256.0 * high + low


def pack_kernel(ids_ref, exp_ref, out_ref, ids_buf, exp_buf, sems):
    a = pltpu.make_async_copy(ids_ref, ids_buf, sems.at[0])
    b = pltpu.make_async_copy(exp_ref, exp_buf, sems.at[1])
    a.start()
    b.start()
    a.wait()
    b.wait()
    out_ref[0] = (exp_buf[...] - 1) + (ids_buf[...] << 16)


def prep_kernel(
    exp_hbm, rates_hbm, emb_hbm, gain_hbm, in_hbm, cw_hbm, cb_hbm, hg_hbm,
    conv_ref, gate_ref, hgt_ref, rate_ref, decay_ref,
    exp_ref, rates_ref, emb_ref, gain_ref, in_ref, cw_ref, cb_ref, hg_ref, sems,
):
    vocab = emb_ref.shape[0]
    inner = hg_ref.shape[1]
    taps = cw_ref.shape[1]
    heads, span = exp_ref.shape
    small = [
        pltpu.make_async_copy(src, dst, sems.at[i])
        for i, (src, dst) in enumerate(
            [
                (exp_hbm, exp_ref), (rates_hbm, rates_ref), (emb_hbm, emb_ref),
                (gain_hbm, gain_ref), (cw_hbm, cw_ref), (cb_hbm, cb_ref), (hg_hbm, hg_ref),
            ]
        )
    ]
    gate_copy = pltpu.make_async_copy(
        in_hbm.at[:, pl.ds(0, inner)], in_ref.at[:, pl.ds(0, inner)], sems.at[7]
    )
    conv_copy = pltpu.make_async_copy(
        in_hbm.at[:, pl.ds(inner, in_ref.shape[1] - inner)],
        in_ref.at[:, pl.ds(inner, in_ref.shape[1] - inner)],
        sems.at[8],
    )
    for copy in small:
        copy.start()
    gate_copy.start()
    conv_copy.start()
    for copy in small:
        copy.wait()

    e = exp_ref[...]
    pre = sums_before(e)
    inc = pre + e.astype(F32)
    rates = jnp.concatenate([rates_ref[...], jnp.zeros((6, heads), F32)], axis=0).T
    half = span // 2
    lower = lax.broadcasted_iota(jnp.int32, (half, half), 0)
    upper = lax.broadcasted_iota(jnp.int32, (half, half), 1)
    zero = jnp.zeros((half, half), BF16)
    for b in range(2):
        rate_ref[b] = jnp.broadcast_to(rates[:, b : b + 1], (heads, span))
        cum = inc if b == 0 else pre
        cum_col = cum.T
        keep = lower <= upper if b == 0 else lower >= upper
        factor = rate_ref[b] * (-LOG2E if b == 0 else LOG2E)
        for h in range(heads):
            for p in range(2):
                for q in range(2):
                    rows = slice(p * half, (p + 1) * half)
                    cols = slice(q * half, (q + 1) * half)
                    if (p > q) if b == 0 else (p < q):
                        decay_ref[b, h, rows, cols] = zero
                        continue
                    gap = cum[h : h + 1, cols] - cum_col[rows, h : h + 1]
                    value = jnp.exp2(gap * factor[h : h + 1, :half])
                    if p == q:
                        value = jnp.where(keep, value, 0.0)
                    decay_ref[b, h, rows, cols] = value.astype(BF16)
    hg = jnp.concatenate([hg_ref[...], jnp.zeros((LANES - 2, inner), F32)], axis=0)
    hgt_ref[...] = hg.T

    em = emb_ref[...].astype(F32)
    norm = em * lax.rsqrt(jnp.mean(em * em, axis=1, keepdims=True) + EPS) * gain_ref[...]
    norm = norm.astype(BF16)
    gate_copy.wait()
    gate = dot(norm, in_ref[:, :inner]).astype(BF16).astype(F32)
    gate = gate / (1.0 + jnp.exp(-gate))
    g0 = gate.astype(BF16)
    g1, g2 = split(gate - g0.astype(F32))
    pad = jnp.zeros((gate_ref.shape[1] - 3 * vocab, inner), BF16)
    gate_ref[...] = jnp.concatenate([g0, g1, g2, pad], axis=0).T
    conv_copy.wait()
    proj = dot(norm, in_ref[:, inner:]).astype(BF16).astype(F32)
    for b in range(2):
        rows = []
        for j in range(taps):
            row = cw_ref[b, j : j + 1, :] * proj
            if j == taps - 1:
                row = row + cb_ref[b : b + 1, :]
            rows.append(0.5 * row)
        high, low = split(jnp.concatenate(rows, axis=0))
        conv_ref[b] = jnp.concatenate([high, low], axis=0).T


def mixer_kernel(
    masks,
    near_ref, far_ref, conv_ref, gate_ref, hgt_ref, rate_ref, decay_ref, out_proj_ref,
    mixed_hbm,
    expo, within, total, ids, shifted, x_held, b_held, state, mixin, mixed, sems,
):
    count = len(masks)
    heads, span = near_ref.shape[1], near_ref.shape[2]
    inner = out_proj_ref.shape[0]
    head = inner // heads
    width = (conv_ref.shape[1] - inner) // 2
    vocab = conv_ref.shape[2] // 8
    me = lax.axis_index("seq")

    for slot, mask in enumerate(masks):
        c = jnp.bitwise_xor(me, mask)
        raw = near_ref[slot] if slot < count // 2 else far_ref[slot - count // 2]
        expo[c] = (raw & 0xFFFF) + 1
        ids[pl.ds(c, 1), :] = raw[0:1] >> 16

    e = expo[...].reshape(count * heads, span)
    pre = sums_before(e)
    within[0] = pre.reshape(count, heads, span)
    inc = pre + e.astype(F32)
    tot = jnp.broadcast_to(inc[:, span - 1 :], inc.shape)
    total[...] = tot.reshape(count, heads, span)
    within[1] = (tot - inc).reshape(count, heads, span)

    tok = ids[...]
    lane = lax.broadcasted_iota(jnp.int32, tok.shape, 1)
    row = lax.broadcasted_iota(jnp.int32, tok.shape, 0)
    for d in range(-3, 4):
        if d == 0:
            moved = tok
        elif d < 0:
            here = pltpu.roll(tok, -d, axis=1)
            other = jnp.where(row == 0, -1, pltpu.roll(here, 1, axis=0))
            moved = jnp.where(lane < -d, other, here)
        else:
            here = pltpu.roll(tok, span - d, axis=1)
            other = jnp.where(row == count - 1, -1, pltpu.roll(here, count - 1, axis=0))
            moved = jnp.where(lane >= span - d, other, here)
        shifted[d + 3] = moved

    values = lax.broadcasted_iota(jnp.int32, (vocab, span), 0)

    def onehot(c, sign):
        rows = []
        for j in range(4):
            token = shifted[3 + (j - 3) * sign, pl.ds(c, 1), :]
            rows.append(jnp.where(values == token, 1.0, 0.0))
        one = jnp.concatenate(rows, axis=0).astype(BF16)
        return jnp.concatenate([one, one], axis=0)

    def convolve(table, one):
        half = dot(table, one)
        return half + half * jnp.tanh(half)

    def remote(i, slot, run):
        rev = i >= me
        b = rev.astype(jnp.int32)
        c = jnp.clip(jnp.where(rev, i + 1, me - 1 - i), 0, count - 1)
        run = jnp.where(i == me, 0.0, run)
        decay = jnp.exp(-rate_ref[b] * (within[1 - b, c] + run))
        one = onehot(c, 1 - 2 * b)
        x = convolve(conv_ref[b, :inner, :], one)
        x = x.reshape(heads, head, span) * decay[:, None, :]
        x_held[slot] = x.reshape(inner, span).astype(BF16)
        bt = convolve(conv_ref[b, inner : inner + width, :], one)
        ahead = jnp.where(rev, 0.0, bt)
        behind = jnp.where(jnp.logical_and(rev, i < count - 1), bt, 0.0)
        b_held[slot] = jnp.concatenate([ahead, behind], axis=0).astype(BF16)
        return run + total[c]

    group = x_held.shape[0]

    def gather(g, run, first):
        for k in range(group):
            run = remote(g * group + k, k, run)
        for r in range(0, inner, 512):
            part = jnp.zeros((512, 2 * width), F32)
            for k in range(group):
                part = part + dot(x_held[k, r : r + 512], b_held[k], NT)
            state[r : r + 512] = part if first else state[r : r + 512] + part
        return run

    run = gather(0, jnp.zeros((heads, span), F32), True)
    if count - 1 > group:
        lax.fori_loop(1, pl.cdiv(count - 1, group), lambda g, run: gather(g, run, False), run)

    own_pre = within[0, me]
    own_inc = own_pre + expo[me].astype(F32)
    own_rest = total[me] - own_pre
    current = jnp.where(values == ids[pl.ds(me, 1), :], 1.0, 0.0).astype(BF16)
    current = jnp.concatenate(
        [current] * 3 + [jnp.zeros((gate_ref.shape[1] - 3 * vocab, span), BF16)], axis=0
    )
    gates = dot(gate_ref[...], current)
    for b in range(2):
        one = onehot(me, 1 - 2 * b)
        conv = convolve(conv_ref[b], one).astype(BF16)
        xt = conv[:inner]
        bt = conv[inner : inner + width]
        ct = conv[inner + width :]
        scores = dot(bt, ct, TN).astype(BF16)
        reach = jnp.exp(-rate_ref[b] * (own_inc if b == 0 else own_rest))
        high, low = split(state[:, b * width : (b + 1) * width])
        carried = dot(
            jnp.concatenate([high, low], axis=1), jnp.concatenate([ct, ct], axis=0)
        )
        for h in range(heads):
            rows = slice(h * head, (h + 1) * head)
            y = dot(xt[rows], scores * decay_ref[b, h])
            y = y + reach[h : h + 1] * carried[rows]
            v = y * gates[rows]
            inv = lax.rsqrt(jnp.sum(v * v, axis=0, keepdims=True) * (1.0 / head) + EPS)
            out = v * inv * hgt_ref[rows, b : b + 1]
            if b == 0:
                mixin[rows] = out
            else:
                mixin[rows] = mixin[rows] + out
    both = mixin[...].astype(BF16).T
    width_out = mixed.shape[1] // 4
    copies = []
    for k in range(4):
        cols = pl.ds(k * width_out, width_out)
        mixed[:, cols] = dot(both, out_proj_ref[:, cols]).astype(BF16)
        copies.append(pltpu.make_async_copy(mixed.at[:, cols], mixed_hbm.at[:, cols], sems.at[k]))
        copies[-1].start()
    for copy in copies:
        copy.wait()


def shards(
    ids, exponents, embedding, norm_gain, in_proj, conv_weight, conv_bias, rates, head_gain, out_proj
):
    count = lax.axis_size("seq")
    bits = count.bit_length() - 1
    heads, span = exponents.shape
    vocab = embedding.shape[0]
    inner = out_proj.shape[0]
    wide = conv_bias.shape[1]
    width = (wide - inner) // 2
    taps = conv_weight.shape[1]
    group = min(count - 1, 16)
    pin = lambda value: pltpu.with_memory_space_constraint(value, pltpu.HBM)
    vmem = pl.BlockSpec(memory_space=pltpu.VMEM)
    hbm = pl.BlockSpec(memory_space=pltpu.HBM)
    f32 = lambda *shape: jax.ShapeDtypeStruct(shape, F32)
    b16 = lambda *shape: jax.ShapeDtypeStruct(shape, BF16)

    packed = pl.pallas_call(
        pack_kernel,
        out_shape=jax.ShapeDtypeStruct((1, heads, span), jnp.int32),
        in_specs=[hbm, hbm],
        out_specs=vmem,
        scratch_shapes=[
            pltpu.VMEM((1, span), jnp.int32),
            pltpu.VMEM((heads, span), jnp.int32),
            pltpu.SemaphoreType.DMA((2,)),
        ],
        compiler_params=pltpu.CompilerParams(vmem_limit_bytes=MIB),
        name="pack",
    )(pin(ids[None, :]), pin(exponents))

    def swap(value, mask):
        return lax.ppermute(value, "seq", [(i, i ^ mask) for i in range(count)])

    stages = [[count // 2, count // 2 + count // 4, count // 4]]
    stages += [[1 << bit] for bit in reversed(range(bits - 2))]
    tables = pl.pallas_call(
        prep_kernel,
        out_shape=(
            b16(2, wide, 2 * taps * vocab),
            b16(inner, LANES),
            f32(inner, LANES),
            f32(2, heads, span),
            b16(2, heads, span, span),
        ),
        in_specs=[hbm] * 8,
        out_specs=(vmem,) * 5,
        scratch_shapes=[
            pltpu.VMEM((heads, span), jnp.int32),
            pltpu.VMEM((2, heads), F32),
            pltpu.VMEM(embedding.shape, BF16),
            pltpu.VMEM((1, inner), F32),
            pltpu.VMEM(in_proj.shape, BF16),
            pltpu.VMEM(conv_weight.shape, F32),
            pltpu.VMEM(conv_bias.shape, F32),
            pltpu.VMEM(head_gain.shape, F32),
            pltpu.SemaphoreType.DMA((9,)),
        ],
        compiler_params=pltpu.CompilerParams(vmem_limit_bytes=16 * MIB),
        name="prep",
        cost_estimate=pl.CostEstimate(
            flops=100_000_000, bytes_accessed=12_000_000, transcendentals=2_000_000
        ),
    )(*map(pin, (exponents, rates, embedding, norm_gain[None, :], in_proj, conv_weight, conv_bias, head_gain)))

    held, masks = packed, [0]
    for k, stage in enumerate(stages[:-1]):
        held = jnp.concatenate([held] + [swap(held, mask) for mask in stage], axis=0)
        masks = masks + [m ^ mask for mask in stage for m in masks]
        if k == 0:
            held, tables = lax.optimization_barrier((held, tables))
    far = swap(held, 1)
    masks = masks + [m ^ 1 for m in masks]

    return pl.pallas_call(
        functools.partial(mixer_kernel, masks),
        out_shape=b16(span, inner),
        in_specs=[vmem] * 8,
        out_specs=hbm,
        scratch_shapes=[
            pltpu.VMEM((count, heads, span), jnp.int32),
            pltpu.VMEM((2, count, heads, span), F32),
            pltpu.VMEM((count, heads, span), F32),
            pltpu.VMEM((count, span), jnp.int32),
            pltpu.VMEM((7, count, span), jnp.int32),
            pltpu.VMEM((group, inner, span), BF16),
            pltpu.VMEM((group, 2 * width, span), BF16),
            pltpu.VMEM((inner, 2 * width), F32),
            pltpu.VMEM((inner, span), F32),
            pltpu.VMEM((span, inner), BF16),
            pltpu.SemaphoreType.DMA((4,)),
        ],
        compiler_params=pltpu.CompilerParams(vmem_limit_bytes=(24 if count <= 32 else 40) * MIB),
        name="mixer",
        cost_estimate=pl.CostEstimate(
            flops=20_000_000_000, bytes_accessed=6_000_000, transcendentals=6_000_000
        ),
    )(held, far, *tables, out_proj)


def solution(mesh):
    in_specs = (
        P(("parts", "seq")),
        P(None, ("parts", "seq")),
        P(), P(), P(), P(), P(), P(), P(), P(),
    )
    out_specs = P(("parts", "seq"), None)
    return jax.shard_map(shards, mesh=mesh, in_specs=in_specs, out_specs=out_specs, check_vma=False)
```

```python
import functools

import jax
import jax.numpy as jnp
from jax import lax
from jax.experimental import pallas as pl
from jax.experimental.pallas import tpu as pltpu
from jax.sharding import PartitionSpec as P

EPS = 1e-05
LOG2E = 1.4426950408889634
F32 = jnp.float32
BF16 = jnp.bfloat16
NT = (((1,), (1,)), ((), ()))
TN = (((0,), (0,)), ((), ()))
MIB = 1024 * 1024
LANES = 128


def dot(a, b, dims=(((1,), (0,)), ((), ()))):
    return lax.dot_general(a, b, dims, preferred_element_type=F32)


def split(value):
    high = value.astype(BF16)
    return high, (value - high.astype(F32)).astype(BF16)


def sums_before(e):
    span = e.shape[1]
    lower = lax.broadcasted_iota(jnp.int32, (span, span), 0)
    upper = lax.broadcasted_iota(jnp.int32, (span, span), 1)
    before = jnp.where(lower < upper, 1.0, 0.0).astype(BF16)
    high = dot((e >> 8).astype(F32).astype(BF16), before)
    low = dot((e & 255).astype(F32).astype(BF16), before)
    return 256.0 * high + low


def convolve(table, one):
    half = dot(table, one)
    return half + half * jnp.tanh(half)


def pack_kernel(ids_ref, exp_ref, out_ref, ids_buf, exp_buf, sems):
    a = pltpu.make_async_copy(ids_ref, ids_buf, sems.at[0])
    b = pltpu.make_async_copy(exp_ref, exp_buf, sems.at[1])
    a.start()
    b.start()
    a.wait()
    b.wait()
    out_ref[0] = (exp_buf[...] - 1) + (ids_buf[...] << 16)


def prep_kernel(
    rates_hbm, emb_hbm, gain_hbm, in_hbm, cw_hbm, cb_hbm, hg_hbm,
    conv_ref, norm_ref, hgt_ref, rate_ref,
    rates_ref, emb_ref, gain_ref, in_ref, cw_ref, cb_ref, hg_ref, sems,
):
    inner = hg_ref.shape[1]
    taps = cw_ref.shape[1]
    heads, span = rate_ref.shape[1:]
    small = [
        pltpu.make_async_copy(src, dst, sems.at[i])
        for i, (src, dst) in enumerate(
            [
                (rates_hbm, rates_ref), (emb_hbm, emb_ref), (gain_hbm, gain_ref),
                (cw_hbm, cw_ref), (cb_hbm, cb_ref), (hg_hbm, hg_ref),
            ]
        )
    ]
    block = in_ref.shape[1] // 2
    wanted = [
        pltpu.make_async_copy(
            in_hbm.at[:, pl.ds(inner + k * block, block)], in_ref.at[:, pl.ds(k * block, block)],
            sems.at[len(small) + k],
        )
        for k in range(2)
    ]
    for copy in small + wanted:
        copy.start()
    for copy in small:
        copy.wait()
    rates = jnp.concatenate([rates_ref[...], jnp.zeros((6, heads), F32)], axis=0).T
    for b in range(2):
        rate_ref[b] = jnp.broadcast_to(rates[:, b : b + 1], (heads, span))
    hg = jnp.concatenate([hg_ref[...], jnp.zeros((LANES - 2, inner), F32)], axis=0)
    hgt_ref[...] = hg.T
    em = emb_ref[...].astype(F32)
    norm = em * lax.rsqrt(jnp.mean(em * em, axis=1, keepdims=True) + EPS) * gain_ref[...]
    norm = norm.astype(BF16)
    norm_ref[...] = norm
    for k, copy in enumerate(wanted):
        copy.wait()
        cols = slice(k * block, (k + 1) * block)
        proj = dot(norm, in_ref[:, cols]).astype(BF16).astype(F32)
        for b in range(2):
            rows = []
            for j in range(taps):
                row = cw_ref[b, j : j + 1, cols] * proj
                if j == taps - 1:
                    row = row + cb_ref[b : b + 1, cols]
                rows.append(0.5 * row)
            high, low = split(jnp.concatenate(rows, axis=0))
            conv_ref[b, cols] = jnp.concatenate([high, low], axis=0).T


def local_kernel(
    held_ref, rate_ref, norm_ref, in_hbm, decay_ref, gates_ref, reach_ref, in_ref, sem
):
    inner = gates_ref.shape[0]
    fetch = pltpu.make_async_copy(in_hbm.at[:, pl.ds(0, inner)], in_ref, sem)
    fetch.start()
    heads, span = held_ref.shape[1:]
    e = (held_ref[0] & 0xFFFF) + 1
    pre = sums_before(e)
    inc = pre + e.astype(F32)
    half = span // 2
    lower = lax.broadcasted_iota(jnp.int32, (half, half), 0)
    upper = lax.broadcasted_iota(jnp.int32, (half, half), 1)
    zero = jnp.zeros((half, half), BF16)
    for b in range(2):
        cum = inc if b == 0 else pre
        cum_col = cum.T
        keep = lower <= upper if b == 0 else lower >= upper
        factor = rate_ref[b] * (-LOG2E if b == 0 else LOG2E)
        for h in range(heads):
            for p in range(2):
                for q in range(2):
                    rows = slice(p * half, (p + 1) * half)
                    cols = slice(q * half, (q + 1) * half)
                    if (p > q) if b == 0 else (p < q):
                        decay_ref[b, h, rows, cols] = zero
                        continue
                    gap = cum[h : h + 1, cols] - cum_col[rows, h : h + 1]
                    value = jnp.exp2(gap * factor[h : h + 1, :half])
                    if p == q:
                        value = jnp.where(keep, value, 0.0)
                    decay_ref[b, h, rows, cols] = value.astype(BF16)
    reach_ref[0] = jnp.exp(-rate_ref[0] * inc)
    reach_ref[1] = jnp.exp(-rate_ref[1] * (inc[:, span - 1 :] - pre))
    vocab = norm_ref.shape[0]
    values = lax.broadcasted_iota(jnp.int32, (vocab, span), 0)
    current = jnp.where(values == (held_ref[0, 0:1] >> 16), 1.0, 0.0).astype(BF16)
    current = jnp.concatenate([current] * 3 + [jnp.zeros_like(current)], axis=0)
    fetch.wait()
    gate = dot(norm_ref[...], in_ref[...]).astype(BF16).astype(F32)
    gate = gate / (1.0 + jnp.exp(-gate))
    g0 = gate.astype(BF16)
    g1, g2 = split(gate - g0.astype(F32))
    gate = jnp.concatenate([g0, g1, g2, jnp.zeros_like(g0)], axis=0)
    gates_ref[...] = dot(gate, current, TN)


def unpack(raw):
    e = (raw & 0xFFFF) + 1
    pre = sums_before(e)
    inc = pre + e.astype(F32)
    tot = jnp.broadcast_to(inc[:, inc.shape[1] - 1 :], inc.shape)
    return pre, tot - inc, tot


def turn_kernel(near_ref, out_ref, turned_ref):
    turned_ref[...] = out_ref[...].T


def states_kernel(
    masks,
    near_ref, far_ref, conv_ref, rate_ref,
    mine_ref, mate_ref, onehot_ref,
    within, total, ids, shifted, x_held, b_held, state,
):
    count = len(masks)
    heads, span = near_ref.shape[1:]
    group, rows, _ = x_held.shape
    width = b_held.shape[1] // 2
    inner = conv_ref.shape[1] - 2 * width
    head = inner // heads
    vocab = conv_ref.shape[2] // 8
    me = lax.axis_index("seq")
    core = me & 1
    base = me - core

    for side, ref in enumerate((near_ref, far_ref)):
        pre, post, tot = unpack(ref[...].reshape(count // 2 * heads, span))
        for slot in range(count // 2):
            c = jnp.bitwise_xor(me, masks[side * (count // 2) + slot])
            block = slice(slot * heads, (slot + 1) * heads)
            within[0, c] = pre[block]
            within[1, c] = post[block]
            total[c] = tot[block]
            ids[pl.ds(c, 1), :] = ref[slot, 0:1] >> 16

    tok = ids[...]
    lane = lax.broadcasted_iota(jnp.int32, tok.shape, 1)
    row = lax.broadcasted_iota(jnp.int32, tok.shape, 0)
    for d in range(-3, 4):
        if d == 0:
            moved = tok
        elif d < 0:
            here = pltpu.roll(tok, -d, axis=1)
            other = jnp.where(row == 0, -1, pltpu.roll(here, 1, axis=0))
            moved = jnp.where(lane < -d, other, here)
        else:
            here = pltpu.roll(tok, span - d, axis=1)
            other = jnp.where(row == count - 1, -1, pltpu.roll(here, count - 1, axis=0))
            moved = jnp.where(lane >= span - d, other, here)
        shifted[d + 3] = moved

    values = lax.broadcasted_iota(jnp.int32, (vocab, span), 0)

    def onehot(c, sign):
        found = []
        for j in range(4):
            token = shifted[3 + (j - 3) * sign, pl.ds(c, 1), :]
            found.append(jnp.where(values == token, 1.0, 0.0))
        one = jnp.concatenate(found, axis=0).astype(BF16)
        return jnp.concatenate([one, one], axis=0)

    first_head = pl.multiple_of(core * (heads // 2), heads // 2)
    first_row = pl.multiple_of(core * rows, rows)
    some = pl.ds(first_head, heads // 2)

    def remote(i, slot, run):
        rev = i >= base
        b = rev.astype(jnp.int32)
        c = jnp.clip(jnp.where(rev, i + 2, base - 1 - i), 0, count - 1)
        run = jnp.where(i == base, 0.0, run)
        dist = within[1 - b, c, some] + run
        decay = jnp.exp(-rate_ref[b, some] * dist)
        one = onehot(c, 1 - 2 * b)
        x = convolve(conv_ref[b, pl.ds(first_row, rows), :], one)
        x = x.reshape(heads // 2, head, span) * decay[:, None, :]
        x_held[slot] = x.reshape(rows, span).astype(BF16)
        bt = convolve(conv_ref[b, inner : inner + width, :], one)
        ahead = jnp.where(rev, 0.0, bt)
        behind = jnp.where(jnp.logical_and(rev, i < count - 2), bt, 0.0)
        b_held[slot] = jnp.concatenate([ahead, behind], axis=0).astype(BF16)
        return run + total[c, some]

    def gather(g, run, first):
        for k in range(group):
            run = remote(g * group + k, k, run)
        part = jnp.zeros((rows, 2 * width), F32)
        for k in range(group):
            part = part + dot(x_held[k], b_held[k], NT)
        state[...] = part if first else state[...] + part
        return run

    run = gather(0, jnp.zeros((heads // 2, span), F32), True)
    if count - 2 > group:
        lax.fori_loop(1, pl.cdiv(count - 2, group), lambda g, run: gather(g, run, False), run)

    stacked = (heads // 2, head, width)
    through, added = [], []
    for b in range(2):
        c = base + b
        one = onehot(c, 1 - 2 * b)
        decay = jnp.exp(-rate_ref[b, some] * within[1 - b, c, some])
        x = convolve(conv_ref[b, pl.ds(first_row, rows), :], one)
        x = x.reshape(heads // 2, head, span) * decay[:, None, :]
        bt = convolve(conv_ref[b, inner : inner + width, :], one)
        added.append(dot(x.reshape(rows, span).astype(BF16), bt.astype(BF16), NT))
        whole = jnp.exp(-rate_ref[b, some] * total[c, some])
        through.append(whole[:, None, :width])
    ahead, behind = state[:, :width], state[:, width:]
    ahead_next = (ahead.reshape(stacked) * through[0]).reshape(rows, width) + added[0]
    behind_next = (behind.reshape(stacked) * through[1]).reshape(rows, width) + added[1]
    first = jnp.concatenate([ahead, behind_next], axis=1).astype(BF16)
    second = jnp.concatenate([ahead_next, behind], axis=1).astype(BF16)
    mine_ref[...] = jnp.where(core == 0, first, second)
    mate_ref[...] = jnp.where(core == 0, second, first)

    onehot_ref[0] = onehot(me, 1)
    onehot_ref[1] = onehot(me, -1)


def own_kernel(
    onehot_ref, conv_ref, decay_ref,
    y_ref, x_ref, scores_ref, c_ref,
):
    inner = y_ref.shape[0]
    width = c_ref.shape[1]
    heads = decay_ref.shape[1]
    head = inner // heads
    for b in range(2):
        conv = convolve(conv_ref[b], onehot_ref[b]).astype(BF16)
        ct = conv[inner + width :]
        c_ref[b] = ct
        scores = dot(conv[inner : inner + width], ct, TN).astype(BF16)
        if b == 1:
            x_ref[...] = conv[:inner]
            scores_ref[...] = scores
            break
        for h in range(heads):
            rows = slice(h * head, (h + 1) * head)
            y_ref[rows] = dot(conv[rows], scores * decay_ref[b, h])


def output_kernel(
    mine_ref, mate_ref, reach_ref, decay_ref,
    y_ref, x_ref, scores_ref, c_ref, gates_ref, hgt_ref, out_ref,
    mixed_hbm,
    state, carried, mixin, mixed, sems,
):
    heads, span = reach_ref.shape[1:]
    inner = y_ref.shape[0]
    width = c_ref.shape[1]
    head = inner // heads
    core = lax.axis_index("seq") & 1
    part = inner // 2
    state[pl.ds(pl.multiple_of(core * part, part), part)] = mine_ref[...]
    state[pl.ds(pl.multiple_of((1 - core) * part, part), part)] = mate_ref[...]
    for b in range(2):
        carried[b] = dot(state[:, b * width : (b + 1) * width], c_ref[b])
    for h in range(heads):
        rows = slice(h * head, (h + 1) * head)
        both = jnp.zeros((head, span), F32)
        for b in range(2):
            if b == 0:
                y = y_ref[rows]
            else:
                y = dot(x_ref[rows], scores_ref[...] * decay_ref[b, h])
            y = y + reach_ref[b, h : h + 1] * carried[b, rows]
            v = y * gates_ref[rows]
            inv = lax.rsqrt(jnp.sum(v * v, axis=0, keepdims=True) * (1.0 / head) + EPS)
            both = both + v * inv * hgt_ref[rows, b : b + 1]
        mixin[rows] = both.astype(BF16)
    columns = mixed.shape[1] // 4
    copies = []
    for k in range(4):
        cols = pl.ds(k * columns, columns)
        mixed[:, cols] = dot(out_ref[cols], mixin[...]).astype(BF16).T
        copies.append(pltpu.make_async_copy(mixed.at[:, cols], mixed_hbm.at[:, cols], sems.at[k]))
        copies[-1].start()
    for copy in copies:
        copy.wait()


def shards(
    ids, exponents, embedding, norm_gain, in_proj, conv_weight, conv_bias, rates, head_gain, out_proj
):
    count = lax.axis_size("seq")
    bits = count.bit_length() - 1
    heads, span = exponents.shape
    vocab = embedding.shape[0]
    inner = out_proj.shape[0]
    wide = conv_bias.shape[1]
    width = (wide - inner) // 2
    taps = conv_weight.shape[1]
    group = min(count - 2, 16)
    pin = lambda value: pltpu.with_memory_space_constraint(value, pltpu.HBM)
    vmem = pl.BlockSpec(memory_space=pltpu.VMEM)
    hbm = pl.BlockSpec(memory_space=pltpu.HBM)
    f32 = lambda *shape: jax.ShapeDtypeStruct(shape, F32)
    b16 = lambda *shape: jax.ShapeDtypeStruct(shape, BF16)

    packed = pl.pallas_call(
        pack_kernel,
        out_shape=jax.ShapeDtypeStruct((1, heads, span), jnp.int32),
        in_specs=[hbm, hbm],
        out_specs=vmem,
        scratch_shapes=[
            pltpu.VMEM((1, span), jnp.int32),
            pltpu.VMEM((heads, span), jnp.int32),
            pltpu.SemaphoreType.DMA((2,)),
        ],
        compiler_params=pltpu.CompilerParams(vmem_limit_bytes=MIB),
        name="pack",
    )(pin(ids[None, :]), pin(exponents))

    def swap(value, mask):
        return lax.ppermute(value, "seq", [(i, i ^ mask) for i in range(count)])

    stages = [[count // 2, count // 2 + count // 4, count // 4]]
    stages += [[1 << bit] for bit in reversed(range(bits - 2))]
    tables = pl.pallas_call(
        prep_kernel,
        out_shape=(
            b16(2, wide, 2 * taps * vocab),
            b16(*embedding.shape),
            f32(inner, LANES),
            f32(2, heads, span),
        ),
        in_specs=[hbm] * 7,
        out_specs=(vmem,) * 4,
        scratch_shapes=[
            pltpu.VMEM((2, heads), F32),
            pltpu.VMEM(embedding.shape, BF16),
            pltpu.VMEM((1, inner), F32),
            pltpu.VMEM((inner, wide), BF16),
            pltpu.VMEM(conv_weight.shape, F32),
            pltpu.VMEM(conv_bias.shape, F32),
            pltpu.VMEM(head_gain.shape, F32),
            pltpu.SemaphoreType.DMA((8,)),
        ],
        compiler_params=pltpu.CompilerParams(vmem_limit_bytes=16 * MIB),
        name="prep",
        cost_estimate=pl.CostEstimate(
            flops=100_000_000, bytes_accessed=12_000_000, transcendentals=2_000_000
        ),
    )(*map(pin, (rates, embedding, norm_gain[None, :], in_proj, conv_weight, conv_bias, head_gain)))

    held, masks = packed, [0]
    for k, stage in enumerate(stages[:-1]):
        held = jnp.concatenate([held] + [swap(held, mask) for mask in stage], axis=0)
        masks = masks + [m ^ mask for mask in stage for m in masks]
        if k == 0:
            held, tables = lax.optimization_barrier((held, tables))
            conv_table, norm_table, gain_table, rate_table = tables
            local = pl.pallas_call(
                local_kernel,
                out_shape=(b16(2, heads, span, span), f32(inner, span), f32(2, heads, span)),
                in_specs=[vmem] * 3 + [hbm],
                out_specs=(vmem,) * 3,
                scratch_shapes=[pltpu.VMEM((inner, inner), BF16), pltpu.SemaphoreType.DMA],
                compiler_params=pltpu.CompilerParams(vmem_limit_bytes=10 * MIB),
                name="local",
                cost_estimate=pl.CostEstimate(
                    flops=20_000_000, bytes_accessed=5_000_000, transcendentals=2_000_000
                ),
            )(held, rate_table, norm_table, pin(in_proj))
        if k == len(stages) - 2:
            held, local = lax.optimization_barrier((held, local))
    far = swap(held, 1)
    masks = masks + [m ^ 1 for m in masks]
    turned = pl.pallas_call(
        turn_kernel,
        out_shape=b16(*out_proj.shape[::-1]),
        in_specs=[hbm, vmem],
        out_specs=vmem,
        compiler_params=pltpu.CompilerParams(vmem_limit_bytes=4 * MIB),
        name="turn",
        cost_estimate=pl.CostEstimate(
            flops=40_000_000, bytes_accessed=6_000_000, transcendentals=0
        ),
    )(held, out_proj)

    decays, gates, reach = local
    mine, mate, onehots = pl.pallas_call(
        functools.partial(states_kernel, masks),
        out_shape=(
            b16(inner // 2, 2 * width), b16(inner // 2, 2 * width),
            b16(2, 2 * taps * vocab, span),
        ),
        in_specs=[vmem] * 4,
        out_specs=(vmem,) * 3,
        scratch_shapes=[
            pltpu.VMEM((2, count, heads, span), F32),
            pltpu.VMEM((count, heads, span), F32),
            pltpu.VMEM((count, span), jnp.int32),
            pltpu.VMEM((7, count, span), jnp.int32),
            pltpu.VMEM((group, inner // 2, span), BF16),
            pltpu.VMEM((group, 2 * width, span), BF16),
            pltpu.VMEM((inner // 2, 2 * width), F32),
        ],
        compiler_params=pltpu.CompilerParams(vmem_limit_bytes=(20 if count <= 32 else 32) * MIB),
        name="states",
        cost_estimate=pl.CostEstimate(
            flops=10_000_000_000, bytes_accessed=4_000_000, transcendentals=3_000_000
        ),
    )(held, far, conv_table, rate_table)
    mate = swap(mate, 1)
    own = pl.pallas_call(
        own_kernel,
        out_shape=(
            f32(inner, span), b16(inner, span), b16(span, span),
            b16(2, width, span),
        ),
        in_specs=[vmem] * 3,
        out_specs=(vmem,) * 4,
        compiler_params=pltpu.CompilerParams(vmem_limit_bytes=12 * MIB),
        name="own",
        cost_estimate=pl.CostEstimate(
            flops=3_000_000_000, bytes_accessed=9_000_000, transcendentals=1_000_000
        ),
    )(onehots, conv_table, decays)
    return pl.pallas_call(
        output_kernel,
        out_shape=b16(span, inner),
        in_specs=[vmem] * 11,
        out_specs=hbm,
        scratch_shapes=[
            pltpu.VMEM((inner, 2 * width), BF16),
            pltpu.VMEM((2, inner, span), F32),
            pltpu.VMEM((inner, span), BF16),
            pltpu.VMEM((span, inner), BF16),
            pltpu.SemaphoreType.DMA((4,)),
        ],
        compiler_params=pltpu.CompilerParams(vmem_limit_bytes=14 * MIB),
        name="output",
        cost_estimate=pl.CostEstimate(
            flops=2_000_000_000, bytes_accessed=6_000_000, transcendentals=100_000
        ),
    )(
        mine, mate, reach, decays, *own, gates, gain_table, turned,
    )


def solution(mesh):
    in_specs = (
        P(("parts", "seq")),
        P(None, ("parts", "seq")),
        P(), P(), P(), P(), P(), P(), P(), P(),
    )
    out_specs = P(("parts", "seq"), None)
    return jax.shard_map(shards, mesh=mesh, in_specs=in_specs, out_specs=out_specs, check_vma=False)
```

```python
import functools

import jax
import jax.numpy as jnp
from jax import lax
from jax.experimental import pallas as pl
from jax.experimental.pallas import tpu as pltpu
from jax.sharding import PartitionSpec as P

EPS = 1e-05
LOG2E = 1.4426950408889634
F32 = jnp.float32
BF16 = jnp.bfloat16
NT = (((1,), (1,)), ((), ()))
TN = (((0,), (0,)), ((), ()))
MIB = 1024 * 1024
LANES = 128


def dot(a, b, dims=(((1,), (0,)), ((), ()))):
    return lax.dot_general(a, b, dims, preferred_element_type=F32)


def split(value):
    high = value.astype(BF16)
    return high, (value - high.astype(F32)).astype(BF16)


def sums_before(e):
    span = e.shape[1]
    lower = lax.broadcasted_iota(jnp.int32, (span, span), 0)
    upper = lax.broadcasted_iota(jnp.int32, (span, span), 1)
    before = jnp.where(lower < upper, 1.0, 0.0).astype(BF16)
    high = dot((e >> 8).astype(F32).astype(BF16), before)
    low = dot((e & 255).astype(F32).astype(BF16), before)
    return 256.0 * high + low


def convolve(table, one):
    half = dot(table, one)
    return half + half * jnp.tanh(half)


def pack_kernel(ids_ref, exp_ref, out_ref, ids_buf, exp_buf, sems):
    a = pltpu.make_async_copy(ids_ref, ids_buf, sems.at[0])
    b = pltpu.make_async_copy(exp_ref, exp_buf, sems.at[1])
    a.start()
    b.start()
    a.wait()
    b.wait()
    out_ref[0] = (exp_buf[...] - 1) + (ids_buf[...] << 16)


def prep_kernel(
    rates_hbm, emb_hbm, gain_hbm, in_hbm, cw_hbm, cb_hbm, hg_hbm,
    conv_ref, norm_ref, hgt_ref, rate_ref,
    rates_ref, emb_ref, gain_ref, in_ref, cw_ref, cb_ref, hg_ref, sems,
):
    inner = hg_ref.shape[1]
    taps = cw_ref.shape[1]
    heads, span = rate_ref.shape[1:]
    small = [
        pltpu.make_async_copy(src, dst, sems.at[i])
        for i, (src, dst) in enumerate(
            [
                (rates_hbm, rates_ref), (emb_hbm, emb_ref), (gain_hbm, gain_ref),
                (cw_hbm, cw_ref), (cb_hbm, cb_ref), (hg_hbm, hg_ref),
            ]
        )
    ]
    block = in_ref.shape[1] // 2
    wanted = [
        pltpu.make_async_copy(
            in_hbm.at[:, pl.ds(inner + k * block, block)], in_ref.at[:, pl.ds(k * block, block)],
            sems.at[len(small) + k],
        )
        for k in range(2)
    ]
    for copy in small + wanted:
        copy.start()
    for copy in small:
        copy.wait()
    rates = jnp.concatenate([rates_ref[...], jnp.zeros((6, heads), F32)], axis=0).T
    for b in range(2):
        rate_ref[b] = jnp.broadcast_to(rates[:, b : b + 1], (heads, span))
    hg = jnp.concatenate([hg_ref[...], jnp.zeros((LANES - 2, inner), F32)], axis=0)
    hgt_ref[...] = hg.T
    em = emb_ref[...].astype(F32)
    norm = em * lax.rsqrt(jnp.mean(em * em, axis=1, keepdims=True) + EPS) * gain_ref[...]
    norm = norm.astype(BF16)
    norm_ref[...] = norm
    for k, copy in enumerate(wanted):
        copy.wait()
        cols = slice(k * block, (k + 1) * block)
        proj = dot(norm, in_ref[:, cols]).astype(BF16).astype(F32)
        for b in range(2):
            rows = []
            for j in range(taps):
                row = cw_ref[b, j : j + 1, cols] * proj
                if j == taps - 1:
                    row = row + cb_ref[b : b + 1, cols]
                rows.append(0.5 * row)
            high, low = split(jnp.concatenate(rows, axis=0))
            conv_ref[b, cols] = jnp.concatenate([high, low], axis=0).T


def local_kernel(
    held_ref, rate_ref, norm_ref, in_hbm, decay_ref, gates_ref, reach_ref, in_ref, sem
):
    inner = gates_ref.shape[0]
    fetch = pltpu.make_async_copy(in_hbm.at[:, pl.ds(0, inner)], in_ref, sem)
    fetch.start()
    heads, span = held_ref.shape[1:]
    e = (held_ref[0] & 0xFFFF) + 1
    pre = sums_before(e)
    inc = pre + e.astype(F32)
    half = span // 2
    lower = lax.broadcasted_iota(jnp.int32, (half, half), 0)
    upper = lax.broadcasted_iota(jnp.int32, (half, half), 1)
    zero = jnp.zeros((half, half), BF16)
    for b in range(2):
        cum = inc if b == 0 else pre
        cum_col = cum.T
        keep = lower <= upper if b == 0 else lower >= upper
        factor = rate_ref[b] * (-LOG2E if b == 0 else LOG2E)
        for h in range(heads):
            for p in range(2):
                for q in range(2):
                    rows = slice(p * half, (p + 1) * half)
                    cols = slice(q * half, (q + 1) * half)
                    if (p > q) if b == 0 else (p < q):
                        decay_ref[b, h, rows, cols] = zero
                        continue
                    gap = cum[h : h + 1, cols] - cum_col[rows, h : h + 1]
                    value = jnp.exp2(gap * factor[h : h + 1, :half])
                    if p == q:
                        value = jnp.where(keep, value, 0.0)
                    decay_ref[b, h, rows, cols] = value.astype(BF16)
    reach_ref[0] = jnp.exp(-rate_ref[0] * inc)
    reach_ref[1] = jnp.exp(-rate_ref[1] * (inc[:, span - 1 :] - pre))
    vocab = norm_ref.shape[0]
    values = lax.broadcasted_iota(jnp.int32, (vocab, span), 0)
    current = jnp.where(values == (held_ref[0, 0:1] >> 16), 1.0, 0.0).astype(BF16)
    current = jnp.concatenate([current] * 3 + [jnp.zeros_like(current)], axis=0)
    fetch.wait()
    gate = dot(norm_ref[...], in_ref[...]).astype(BF16).astype(F32)
    gate = gate / (1.0 + jnp.exp(-gate))
    g0 = gate.astype(BF16)
    g1, g2 = split(gate - g0.astype(F32))
    gate = jnp.concatenate([g0, g1, g2, jnp.zeros_like(g0)], axis=0)
    gates_ref[...] = dot(gate, current, TN)


def unpack(raw):
    e = (raw & 0xFFFF) + 1
    pre = sums_before(e)
    inc = pre + e.astype(F32)
    tot = jnp.broadcast_to(inc[:, inc.shape[1] - 1 :], inc.shape)
    return pre, tot - inc, tot


def shift_tokens(ids, shifted):
    tok = ids[...]
    count, span = tok.shape
    lane = lax.broadcasted_iota(jnp.int32, tok.shape, 1)
    row = lax.broadcasted_iota(jnp.int32, tok.shape, 0)
    for d in range(-3, 4):
        if d == 0:
            moved = tok
        elif d < 0:
            here = pltpu.roll(tok, -d, axis=1)
            other = jnp.where(row == 0, -1, pltpu.roll(here, 1, axis=0))
            moved = jnp.where(lane < -d, other, here)
        else:
            here = pltpu.roll(tok, span - d, axis=1)
            other = jnp.where(row == count - 1, -1, pltpu.roll(here, count - 1, axis=0))
            moved = jnp.where(lane >= span - d, other, here)
        shifted[d + 3] = moved


def turn_kernel(near_ref, out_ref, turned_ref):
    turned_ref[...] = out_ref[...].T


def states_kernel(
    masks,
    near_ref, far_ref, conv_ref, rate_ref,
    mine_ref, mate_ref, onehot_ref,
    within, total, ids, shifted, x_held, b_held, state,
):
    count = len(masks)
    heads, span = near_ref.shape[1:]
    group, rows, _ = x_held.shape
    width = b_held.shape[1] // 2
    inner = conv_ref.shape[1] - 2 * width
    head = inner // heads
    vocab = conv_ref.shape[2] // 8
    me = lax.axis_index("seq")
    core = me & 1
    base = me - core

    for side, ref in enumerate((near_ref, far_ref)):
        pre, post, tot = unpack(ref[...].reshape(count // 2 * heads, span))
        for slot in range(count // 2):
            c = jnp.bitwise_xor(me, masks[side * (count // 2) + slot])
            block = slice(slot * heads, (slot + 1) * heads)
            within[0, c] = pre[block]
            within[1, c] = post[block]
            total[c] = tot[block]
            ids[pl.ds(c, 1), :] = ref[slot, 0:1] >> 16

    shift_tokens(ids, shifted)
    values = lax.broadcasted_iota(jnp.int32, (vocab, span), 0)

    def onehot(c, sign):
        found = []
        for j in range(4):
            token = shifted[3 + (j - 3) * sign, pl.ds(c, 1), :]
            found.append(jnp.where(values == token, 1.0, 0.0))
        one = jnp.concatenate(found, axis=0).astype(BF16)
        return jnp.concatenate([one, one], axis=0)

    first_head = pl.multiple_of(core * (heads // 2), heads // 2)
    first_row = pl.multiple_of(core * rows, rows)
    some = pl.ds(first_head, heads // 2)

    def remote(i, slot, run):
        rev = i >= base
        b = rev.astype(jnp.int32)
        c = jnp.clip(jnp.where(rev, i + 2, base - 1 - i), 0, count - 1)
        run = jnp.where(i == base, 0.0, run)
        dist = within[1 - b, c, some] + run
        decay = jnp.exp(-rate_ref[b, some] * dist)
        one = onehot(c, 1 - 2 * b)
        x = convolve(conv_ref[b, pl.ds(first_row, rows), :], one)
        x = x.reshape(heads // 2, head, span) * decay[:, None, :]
        x_held[slot] = x.reshape(rows, span).astype(BF16)
        bt = convolve(conv_ref[b, inner : inner + width, :], one)
        ahead = jnp.where(rev, 0.0, bt)
        behind = jnp.where(jnp.logical_and(rev, i < count - 2), bt, 0.0)
        b_held[slot] = jnp.concatenate([ahead, behind], axis=0).astype(BF16)
        return run + total[c, some]

    def gather(g, run, first):
        for k in range(group):
            run = remote(g * group + k, k, run)
        part = jnp.zeros((rows, 2 * width), F32)
        for k in range(group):
            part = part + dot(x_held[k], b_held[k], NT)
        state[...] = part if first else state[...] + part
        return run

    run = gather(0, jnp.zeros((heads // 2, span), F32), True)
    if count - 2 > group:
        lax.fori_loop(1, pl.cdiv(count - 2, group), lambda g, run: gather(g, run, False), run)

    stacked = (heads // 2, head, width)
    through, added = [], []
    for b in range(2):
        c = base + b
        one = onehot(c, 1 - 2 * b)
        decay = jnp.exp(-rate_ref[b, some] * within[1 - b, c, some])
        x = convolve(conv_ref[b, pl.ds(first_row, rows), :], one)
        x = x.reshape(heads // 2, head, span) * decay[:, None, :]
        bt = convolve(conv_ref[b, inner : inner + width, :], one)
        added.append(dot(x.reshape(rows, span).astype(BF16), bt.astype(BF16), NT))
        whole = jnp.exp(-rate_ref[b, some] * total[c, some])
        through.append(whole[:, None, :width])
    ahead, behind = state[:, :width], state[:, width:]
    ahead_next = (ahead.reshape(stacked) * through[0]).reshape(rows, width) + added[0]
    behind_next = (behind.reshape(stacked) * through[1]).reshape(rows, width) + added[1]
    first = jnp.concatenate([ahead, behind_next], axis=1).astype(BF16)
    second = jnp.concatenate([ahead_next, behind], axis=1).astype(BF16)
    mine_ref[...] = jnp.where(core == 0, first, second)
    mate_ref[...] = jnp.where(core == 0, second, first)

    onehot_ref[0] = onehot(me, 1)
    onehot_ref[1] = onehot(me, -1)


def spans_kernel(
    first, masks, held_ref, conv_ref, rate_ref, state_ref, within_ref, total_ref, x_held, b_held
):
    heads, span = held_ref.shape[1:]
    count, inner, width = state_ref.shape
    head = inner // heads
    vocab = conv_ref.shape[2] // 8
    me = lax.axis_index("seq")
    pre, post, tot = unpack(held_ref[first : first + count].reshape(count * heads, span))
    within_ref[0] = pre.reshape(count, heads, span)
    within_ref[1] = post.reshape(count, heads, span)
    total_ref[...] = tot.reshape(count, heads, span)
    lane = lax.broadcasted_iota(jnp.int32, (heads, span), 1)
    values = lax.broadcasted_iota(jnp.int32, (vocab, span), 0)
    for k, mask in enumerate(masks):
        rev = (jnp.bitwise_xor(me, mask) > me) if mask else (me & 1) == 1
        b = rev.astype(jnp.int32)
        token = jnp.broadcast_to(held_ref[first + k, 0:1] >> 16, (vocab, span))
        found = []
        for far in (3, 2, 1, 0):
            there = token
            if far:
                there = jnp.where(rev, pltpu.roll(token, span - far, 1), pltpu.roll(token, far, 1))
            found.append(jnp.where(values == there, 1.0, 0.0))
        one = jnp.concatenate(found, axis=0).astype(BF16)
        one = jnp.concatenate([one, one], axis=0)
        rows = slice(k * heads, (k + 1) * heads)
        decay = jnp.exp(-rate_ref[b] * jnp.where(rev, pre[rows], post[rows]))
        decay = jnp.where(jnp.where(rev, span - 1 - lane, lane) < 3, 0.0, decay)
        x = convolve(conv_ref[b, :inner, :], one).reshape(heads, head, span) * decay[:, None, :]
        bt = convolve(conv_ref[b, inner : inner + width, :], one)
        x_held[k] = x.reshape(inner, span).astype(BF16)
        b_held[k] = bt.astype(BF16)
    for k in range(count):
        for r in range(0, inner, 512):
            state_ref[k, r : r + 512] = dot(x_held[k, r : r + 512], b_held[k], NT)


def combine_kernel(
    masks,
    held_ref, far_ref, state_a, within_a, total_a, state_b, within_b, total_b, conv_ref, rate_ref,
    mine_ref, mate_ref, onehot_ref,
    totals, between, ids, shifted,
):
    count = 2 * len(masks)
    heads, span = held_ref.shape[1:]
    first, inner, width = state_a.shape
    head = inner // heads
    vocab = conv_ref.shape[2] // 8
    me = lax.axis_index("seq")
    core = me & 1
    base = me - core
    parts = [(state_a, within_a, total_a, k) for k in range(first)]
    parts += [(state_b, within_b, total_b, k) for k in range(len(masks) - first)]

    far_e = ((far_ref[...].reshape(len(masks) * heads, span) & 0xFFFF) + 1).astype(F32)
    far_tot = jnp.broadcast_to(jnp.sum(far_e, axis=1, keepdims=True), (len(masks) * heads, LANES))
    for slot, mask in enumerate(masks):
        c = jnp.bitwise_xor(me, mask)
        _, _, tot, k = parts[slot]
        totals[c] = tot[k, :, :LANES]
        ids[pl.ds(c, 1), :] = held_ref[slot, 0:1] >> 16
        c = jnp.bitwise_xor(c, 1)
        totals[c] = far_tot[slot * heads : (slot + 1) * heads]
        ids[pl.ds(c, 1), :] = far_ref[slot, 0:1] >> 16
    run = jnp.zeros((heads, LANES), F32)
    for i in range(count - 2):
        c = jnp.where(i >= base, i + 2, base - 1 - i)
        run = jnp.where(i == base, 0.0, run)
        between[c] = run
        run = run + totals[c]
    between[me] = jnp.zeros((heads, LANES), F32)

    shift_tokens(ids, shifted)
    values = lax.broadcasted_iota(jnp.int32, (vocab, span), 0)
    for b in range(2):
        found = []
        for j in range(4):
            token = shifted[j if b == 0 else 6 - j, pl.ds(me, 1), :]
            found.append(jnp.where(values == token, 1.0, 0.0))
        one = jnp.concatenate(found, axis=0).astype(BF16)
        onehot_ref[b] = jnp.concatenate([one, one], axis=0)

    lane = lax.broadcasted_iota(jnp.int32, (1, span), 1)
    token = jnp.full((8, span), -1, jnp.int32)
    kind = jnp.full((1, span), -1, jnp.int32)
    side = jnp.full((1, span), -1, jnp.int32)
    dist = jnp.zeros((heads, LANES), F32)
    rate = jnp.zeros((heads, LANES), F32)
    scales = []
    for slot, mask in enumerate(masks):
        c = jnp.bitwise_xor(me, mask)
        rev = (c > me) if mask else core == 1
        b = rev.astype(jnp.int32)
        here = jnp.logical_and(lane >= 8 * slot, lane < 8 * slot + 3)
        near = here[:, :LANES]
        taps = jnp.concatenate(
            [shifted[3 + (j - 3) * (1 - 2 * b), pl.ds(c, 1), :] for j in (0, 1, 2, 3, 0, 1, 2, 3)],
            axis=0,
        )

        def moved(ahead, behind):
            start = ahead if slot == 0 else pltpu.roll(ahead, 8 * slot, 1)
            return jnp.where(rev, pltpu.roll(behind, 8 * slot + 3, 1), start)

        token = jnp.where(here, moved(taps, taps), token)
        side = jnp.where(here, b, side)
        kind = jnp.where(here, b if mask else 2, kind)
        _, within, _, k = parts[slot]
        gap = moved(within[1, k], within[0, k])[:, :LANES] + between[c]
        dist = jnp.where(near, gap, dist)
        rate = jnp.where(near, rate_ref[b, :, :LANES], rate)
        scale = jnp.exp(-rate_ref[b, :, :LANES] * between[c])
        scales.append((jnp.where(rev, 0.0, scale), jnp.where(rev, scale, 0.0)))
    values = values[:, :LANES]
    found = [jnp.where(values == token[j : j + 1, :LANES], 1.0, 0.0) for j in range(4)]
    one = jnp.concatenate(found, axis=0)
    side, kind = side[:, :LANES], kind[:, :LANES]
    ones = [jnp.where(side == b, one, 0.0).astype(BF16) for b in (0, 0, 1, 1)]
    table = jnp.concatenate(
        [conv_ref[0, : inner + width, :], conv_ref[1, : inner + width, :]], axis=1
    )
    conv = convolve(table, jnp.concatenate(ones, axis=0))
    x = conv[:inner].reshape(heads, head, LANES) * jnp.exp(-rate * dist)[:, None, :]
    bt = conv[inner:]
    bt = jnp.concatenate([jnp.where(kind == i, bt, 0.0) for i in range(3)], axis=0)
    edges = dot(x.reshape(inner, LANES).astype(BF16), bt.astype(BF16), NT)

    through = [jnp.exp(-rate_ref[b, :, :LANES] * totals[base + b]) for b in range(2)]
    for h in range(heads):
        rows = slice(h * head, (h + 1) * head)
        ahead, behind = edges[rows, :width], edges[rows, width : 2 * width]
        own = edges[rows, 2 * width :]
        for slot, mask in enumerate(masks):
            state, _, _, k = parts[slot]
            value = state[k, rows]
            if not mask:
                own = own + value
                continue
            ahead = ahead + value * scales[slot][0][h : h + 1]
            behind = behind + value * scales[slot][1][h : h + 1]
        ahead_next = ahead * through[0][h : h + 1]
        behind_next = behind * through[1][h : h + 1]
        zero = core == 0
        mine_ref[rows, :width] = jnp.where(zero, ahead, ahead_next)
        mine_ref[rows, width:] = jnp.where(zero, behind_next, behind)
        mate_ref[rows, :width] = jnp.where(zero, ahead_next + own, ahead).astype(BF16)
        mate_ref[rows, width:] = jnp.where(zero, behind, behind_next + own).astype(BF16)


def own_kernel(
    onehot_ref, conv_ref, decay_ref,
    y_ref, x_ref, scores_ref, c_ref,
):
    inner = y_ref.shape[0]
    width = c_ref.shape[1]
    heads = decay_ref.shape[1]
    head = inner // heads
    for b in range(2):
        conv = convolve(conv_ref[b], onehot_ref[b]).astype(BF16)
        ct = conv[inner + width :]
        c_ref[b] = ct
        scores = dot(conv[inner : inner + width], ct, TN).astype(BF16)
        if b == 1:
            x_ref[...] = conv[:inner]
            scores_ref[...] = scores
            break
        for h in range(heads):
            rows = slice(h * head, (h + 1) * head)
            y_ref[rows] = dot(conv[rows], scores * decay_ref[b, h])


def output_kernel(
    summed,
    mine_ref, mate_ref, reach_ref, decay_ref,
    y_ref, x_ref, scores_ref, c_ref, gates_ref, hgt_ref, out_ref,
    mixed_hbm,
    state, carried, mixin, mixed, sems,
):
    heads, span = reach_ref.shape[1:]
    inner = y_ref.shape[0]
    width = c_ref.shape[1]
    head = inner // heads
    core = lax.axis_index("seq") & 1
    part = inner // 2
    if summed:
        state[...] = (mine_ref[...] + mate_ref[...].astype(F32)).astype(BF16)
    else:
        state[pl.ds(pl.multiple_of(core * part, part), part)] = mine_ref[...]
        state[pl.ds(pl.multiple_of((1 - core) * part, part), part)] = mate_ref[...]
    for b in range(2):
        carried[b] = dot(state[:, b * width : (b + 1) * width], c_ref[b])
    for h in range(heads):
        rows = slice(h * head, (h + 1) * head)
        both = jnp.zeros((head, span), F32)
        for b in range(2):
            if b == 0:
                y = y_ref[rows]
            else:
                y = dot(x_ref[rows], scores_ref[...] * decay_ref[b, h])
            y = y + reach_ref[b, h : h + 1] * carried[b, rows]
            v = y * gates_ref[rows]
            inv = lax.rsqrt(jnp.sum(v * v, axis=0, keepdims=True) * (1.0 / head) + EPS)
            both = both + v * inv * hgt_ref[rows, b : b + 1]
        mixin[rows] = both.astype(BF16)
    columns = mixed.shape[1] // 4
    copies = []
    for k in range(4):
        cols = pl.ds(k * columns, columns)
        mixed[:, cols] = dot(out_ref[cols], mixin[...]).astype(BF16).T
        copies.append(pltpu.make_async_copy(mixed.at[:, cols], mixed_hbm.at[:, cols], sems.at[k]))
        copies[-1].start()
    for copy in copies:
        copy.wait()


def shards(
    ids, exponents, embedding, norm_gain, in_proj, conv_weight, conv_bias, rates, head_gain, out_proj
):
    count = lax.axis_size("seq")
    bits = count.bit_length() - 1
    heads, span = exponents.shape
    vocab = embedding.shape[0]
    inner = out_proj.shape[0]
    wide = conv_bias.shape[1]
    width = (wide - inner) // 2
    taps = conv_weight.shape[1]
    group = min(count - 2, 16)
    pin = lambda value: pltpu.with_memory_space_constraint(value, pltpu.HBM)
    vmem = pl.BlockSpec(memory_space=pltpu.VMEM)
    hbm = pl.BlockSpec(memory_space=pltpu.HBM)
    f32 = lambda *shape: jax.ShapeDtypeStruct(shape, F32)
    b16 = lambda *shape: jax.ShapeDtypeStruct(shape, BF16)

    packed = pl.pallas_call(
        pack_kernel,
        out_shape=jax.ShapeDtypeStruct((1, heads, span), jnp.int32),
        in_specs=[hbm, hbm],
        out_specs=vmem,
        scratch_shapes=[
            pltpu.VMEM((1, span), jnp.int32),
            pltpu.VMEM((heads, span), jnp.int32),
            pltpu.SemaphoreType.DMA((2,)),
        ],
        compiler_params=pltpu.CompilerParams(vmem_limit_bytes=MIB),
        name="pack",
    )(pin(ids[None, :]), pin(exponents))

    def swap(value, mask):
        return lax.ppermute(value, "seq", [(i, i ^ mask) for i in range(count)])

    stages = [[count // 2, count // 2 + count // 4, count // 4]]
    stages += [[1 << bit] for bit in reversed(range(bits - 2))]
    tables = pl.pallas_call(
        prep_kernel,
        out_shape=(
            b16(2, wide, 2 * taps * vocab),
            b16(*embedding.shape),
            f32(inner, LANES),
            f32(2, heads, span),
        ),
        in_specs=[hbm] * 7,
        out_specs=(vmem,) * 4,
        scratch_shapes=[
            pltpu.VMEM((2, heads), F32),
            pltpu.VMEM(embedding.shape, BF16),
            pltpu.VMEM((1, inner), F32),
            pltpu.VMEM((inner, wide), BF16),
            pltpu.VMEM(conv_weight.shape, F32),
            pltpu.VMEM(conv_bias.shape, F32),
            pltpu.VMEM(head_gain.shape, F32),
            pltpu.SemaphoreType.DMA((8,)),
        ],
        compiler_params=pltpu.CompilerParams(vmem_limit_bytes=16 * MIB),
        name="prep",
        cost_estimate=pl.CostEstimate(
            flops=100_000_000, bytes_accessed=12_000_000, transcendentals=2_000_000
        ),
    )(*map(pin, (rates, embedding, norm_gain[None, :], in_proj, conv_weight, conv_bias, head_gain)))

    conv_table, norm_table, gain_table, rate_table = tables
    local = pl.pallas_call(
        local_kernel,
        out_shape=(b16(2, heads, span, span), f32(inner, span), f32(2, heads, span)),
        in_specs=[vmem] * 3 + [hbm],
        out_specs=(vmem,) * 3,
        scratch_shapes=[pltpu.VMEM((inner, inner), BF16), pltpu.SemaphoreType.DMA],
        compiler_params=pltpu.CompilerParams(vmem_limit_bytes=10 * MIB),
        name="local",
        cost_estimate=pl.CostEstimate(
            flops=20_000_000, bytes_accessed=5_000_000, transcendentals=2_000_000
        ),
    )(packed, rate_table, norm_table, pin(in_proj))

    def spans(first, some, held):
        many = len(some)
        return pl.pallas_call(
            functools.partial(spans_kernel, first, some),
            out_shape=(
                f32(many, inner, width), f32(2, many, heads, span), f32(many, heads, span),
            ),
            in_specs=[vmem] * 3,
            out_specs=(vmem,) * 3,
            scratch_shapes=[
                pltpu.VMEM((many, inner, span), BF16), pltpu.VMEM((many, width, span), BF16),
            ],
            compiler_params=pltpu.CompilerParams(vmem_limit_bytes=12 * MIB),
            name="spans",
            cost_estimate=pl.CostEstimate(
                flops=2_000_000_000, bytes_accessed=4_000_000, transcendentals=1_000_000
            ),
        )(held, conv_table, rate_table)

    def turn(value):
        return pl.pallas_call(
            turn_kernel,
            out_shape=b16(*out_proj.shape[::-1]),
            in_specs=[hbm, vmem],
            out_specs=vmem,
            compiler_params=pltpu.CompilerParams(vmem_limit_bytes=4 * MIB),
            name="turn",
            cost_estimate=pl.CostEstimate(
                flops=40_000_000, bytes_accessed=6_000_000, transcendentals=0
            ),
        )(value, out_proj)

    summed = count == 16
    held, masks, early = packed, [0], []
    for k, stage in enumerate(stages[:-1]):
        if k == 1:
            held, local = lax.optimization_barrier((held, local))
        new = [swap(held, mask) for mask in stage]
        if k == 1:
            turned = turn(held)
            if summed:
                early.append(spans(0, masks, held))
        held = jnp.concatenate([held] + new, axis=0)
        masks = masks + [m ^ mask for mask in stage for m in masks]
        if k == 1:
            held, early, turned = lax.optimization_barrier((held, early, turned))
    far = swap(held, 1)
    if summed:
        early.append(spans(len(masks) // 2, masks[len(masks) // 2 :], held))
    decays, gates, reach = local
    if summed:
        mine, mate, onehots = pl.pallas_call(
            functools.partial(combine_kernel, masks),
            out_shape=(f32(inner, 2 * width), b16(inner, 2 * width), b16(2, 2 * taps * vocab, span)),
            in_specs=[vmem] * 10,
            out_specs=(vmem,) * 3,
            scratch_shapes=[
                pltpu.VMEM((count, heads, LANES), F32),
                pltpu.VMEM((count, heads, LANES), F32),
                pltpu.VMEM((count, span), jnp.int32),
                pltpu.VMEM((7, count, span), jnp.int32),
            ],
            compiler_params=pltpu.CompilerParams(vmem_limit_bytes=12 * MIB),
            name="combine",
            cost_estimate=pl.CostEstimate(
                flops=1_000_000_000, bytes_accessed=8_000_000, transcendentals=300_000
            ),
        )(held, far, *early[0], *early[1], conv_table, rate_table)
    else:
        masks = masks + [m ^ 1 for m in masks]
        mine, mate, onehots = pl.pallas_call(
            functools.partial(states_kernel, masks),
            out_shape=(
                b16(inner // 2, 2 * width), b16(inner // 2, 2 * width),
                b16(2, 2 * taps * vocab, span),
            ),
            in_specs=[vmem] * 4,
            out_specs=(vmem,) * 3,
            scratch_shapes=[
                pltpu.VMEM((2, count, heads, span), F32),
                pltpu.VMEM((count, heads, span), F32),
                pltpu.VMEM((count, span), jnp.int32),
                pltpu.VMEM((7, count, span), jnp.int32),
                pltpu.VMEM((group, inner // 2, span), BF16),
                pltpu.VMEM((group, 2 * width, span), BF16),
                pltpu.VMEM((inner // 2, 2 * width), F32),
            ],
            compiler_params=pltpu.CompilerParams(vmem_limit_bytes=(20 if count <= 32 else 32) * MIB),
            name="states",
            cost_estimate=pl.CostEstimate(
                flops=10_000_000_000, bytes_accessed=4_000_000, transcendentals=3_000_000
            ),
        )(held, far, conv_table, rate_table)
    mate = swap(mate, 1)
    own = pl.pallas_call(
        own_kernel,
        out_shape=(
            f32(inner, span), b16(inner, span), b16(span, span),
            b16(2, width, span),
        ),
        in_specs=[vmem] * 3,
        out_specs=(vmem,) * 4,
        compiler_params=pltpu.CompilerParams(vmem_limit_bytes=12 * MIB),
        name="own",
        cost_estimate=pl.CostEstimate(
            flops=3_000_000_000, bytes_accessed=9_000_000, transcendentals=1_000_000
        ),
    )(onehots, conv_table, decays)
    return pl.pallas_call(
        functools.partial(output_kernel, summed),
        out_shape=b16(span, inner),
        in_specs=[vmem] * 11,
        out_specs=hbm,
        scratch_shapes=[
            pltpu.VMEM((inner, 2 * width), BF16),
            pltpu.VMEM((2, inner, span), F32),
            pltpu.VMEM((inner, span), BF16),
            pltpu.VMEM((span, inner), BF16),
            pltpu.SemaphoreType.DMA((4,)),
        ],
        compiler_params=pltpu.CompilerParams(vmem_limit_bytes=14 * MIB),
        name="output",
        cost_estimate=pl.CostEstimate(
            flops=2_000_000_000, bytes_accessed=6_000_000, transcendentals=100_000
        ),
    )(
        mine, mate, reach, decays, *own, gates, gain_table, turned,
    )


def solution(mesh):
    in_specs = (
        P(("parts", "seq")),
        P(None, ("parts", "seq")),
        P(), P(), P(), P(), P(), P(), P(), P(),
    )
    out_specs = P(("parts", "seq"), None)
    return jax.shard_map(shards, mesh=mesh, in_specs=in_specs, out_specs=out_specs, check_vma=False)
```

```python
import functools

import jax
import jax.numpy as jnp
from jax import lax
from jax.experimental import pallas as pl
from jax.experimental.pallas import tpu as pltpu
from jax.sharding import PartitionSpec as P

EPS = 1e-05
LOG2E = 1.4426950408889634
F32 = jnp.float32
BF16 = jnp.bfloat16
NT = (((1,), (1,)), ((), ()))
TN = (((0,), (0,)), ((), ()))
MIB = 1024 * 1024
LANES = 128


def dot(a, b, dims=(((1,), (0,)), ((), ()))):
    return lax.dot_general(a, b, dims, preferred_element_type=F32)


def split(value):
    high = value.astype(BF16)
    return high, (value - high.astype(F32)).astype(BF16)


def sums_before(e):
    span = e.shape[1]
    lower = lax.broadcasted_iota(jnp.int32, (span, span), 0)
    upper = lax.broadcasted_iota(jnp.int32, (span, span), 1)
    before = jnp.where(lower < upper, 1.0, 0.0).astype(BF16)
    high = dot((e >> 8).astype(F32).astype(BF16), before)
    low = dot((e & 255).astype(F32).astype(BF16), before)
    return 256.0 * high + low


def convolve(table, one):
    half = dot(table, one)
    return half + half * jnp.tanh(half)


def pack_kernel(ids_ref, exp_ref, out_ref, ids_buf, exp_buf, sems):
    a = pltpu.make_async_copy(ids_ref, ids_buf, sems.at[0])
    b = pltpu.make_async_copy(exp_ref, exp_buf, sems.at[1])
    a.start()
    b.start()
    a.wait()
    b.wait()
    out_ref[0] = (exp_buf[...] - 1) + (ids_buf[...] << 16)


def prep_kernel(
    rates_hbm, emb_hbm, gain_hbm, in_hbm, cw_hbm, cb_hbm, hg_hbm,
    conv_ref, norm_ref, hgt_ref, rate_ref,
    rates_ref, emb_ref, gain_ref, in_ref, cw_ref, cb_ref, hg_ref, sems,
):
    inner = hg_ref.shape[1]
    taps = cw_ref.shape[1]
    heads, span = rate_ref.shape[1:]
    small = [
        pltpu.make_async_copy(src, dst, sems.at[i])
        for i, (src, dst) in enumerate(
            [
                (rates_hbm, rates_ref), (emb_hbm, emb_ref), (gain_hbm, gain_ref),
                (cw_hbm, cw_ref), (cb_hbm, cb_ref), (hg_hbm, hg_ref),
            ]
        )
    ]
    block = in_ref.shape[1] // 2
    wanted = [
        pltpu.make_async_copy(
            in_hbm.at[:, pl.ds(inner + k * block, block)], in_ref.at[:, pl.ds(k * block, block)],
            sems.at[len(small) + k],
        )
        for k in range(2)
    ]
    for copy in small + wanted:
        copy.start()
    for copy in small:
        copy.wait()
    rates = jnp.concatenate([rates_ref[...], jnp.zeros((6, heads), F32)], axis=0).T
    for b in range(2):
        rate_ref[b] = jnp.broadcast_to(rates[:, b : b + 1], (heads, span))
    hg = jnp.concatenate([hg_ref[...], jnp.zeros((LANES - 2, inner), F32)], axis=0)
    hgt_ref[...] = hg.T
    em = emb_ref[...].astype(F32)
    norm = em * lax.rsqrt(jnp.mean(em * em, axis=1, keepdims=True) + EPS) * gain_ref[...]
    norm = norm.astype(BF16)
    norm_ref[...] = norm
    for k, copy in enumerate(wanted):
        copy.wait()
        cols = slice(k * block, (k + 1) * block)
        proj = dot(norm, in_ref[:, cols]).astype(BF16).astype(F32)
        for b in range(2):
            rows = []
            for j in range(taps):
                row = cw_ref[b, j : j + 1, cols] * proj
                if j == taps - 1:
                    row = row + cb_ref[b : b + 1, cols]
                rows.append(0.5 * row)
            high, low = split(jnp.concatenate(rows, axis=0))
            conv_ref[b, cols] = jnp.concatenate([high, low], axis=0).T


def local_kernel(
    held_ref, rate_ref, norm_ref, in_hbm, decay_ref, gates_ref, reach_ref, in_ref, sem
):
    inner = gates_ref.shape[0]
    fetch = pltpu.make_async_copy(in_hbm.at[:, pl.ds(0, inner)], in_ref, sem)
    fetch.start()
    heads, span = held_ref.shape[1:]
    e = (held_ref[0] & 0xFFFF) + 1
    pre = sums_before(e)
    inc = pre + e.astype(F32)
    half = span // 2
    lower = lax.broadcasted_iota(jnp.int32, (half, half), 0)
    upper = lax.broadcasted_iota(jnp.int32, (half, half), 1)
    zero = jnp.zeros((half, half), BF16)
    for b in range(2):
        cum = inc if b == 0 else pre
        cum_col = cum.T
        keep = lower <= upper if b == 0 else lower >= upper
        factor = rate_ref[b] * (-LOG2E if b == 0 else LOG2E)
        for h in range(heads):
            for p in range(2):
                for q in range(2):
                    rows = slice(p * half, (p + 1) * half)
                    cols = slice(q * half, (q + 1) * half)
                    if (p > q) if b == 0 else (p < q):
                        decay_ref[b, h, rows, cols] = zero
                        continue
                    gap = cum[h : h + 1, cols] - cum_col[rows, h : h + 1]
                    value = jnp.exp2(gap * factor[h : h + 1, :half])
                    if p == q:
                        value = jnp.where(keep, value, 0.0)
                    decay_ref[b, h, rows, cols] = value.astype(BF16)
    reach_ref[0] = jnp.exp(-rate_ref[0] * inc)
    reach_ref[1] = jnp.exp(-rate_ref[1] * (inc[:, span - 1 :] - pre))
    vocab = norm_ref.shape[0]
    values = lax.broadcasted_iota(jnp.int32, (vocab, span), 0)
    current = jnp.where(values == (held_ref[0, 0:1] >> 16), 1.0, 0.0).astype(BF16)
    current = jnp.concatenate([current] * 3 + [jnp.zeros_like(current)], axis=0)
    fetch.wait()
    gate = dot(norm_ref[...], in_ref[...]).astype(BF16).astype(F32)
    gate = gate / (1.0 + jnp.exp(-gate))
    g0 = gate.astype(BF16)
    g1, g2 = split(gate - g0.astype(F32))
    gate = jnp.concatenate([g0, g1, g2, jnp.zeros_like(g0)], axis=0)
    gates_ref[...] = dot(gate, current, TN)


def unpack(raw):
    e = (raw & 0xFFFF) + 1
    pre = sums_before(e)
    inc = pre + e.astype(F32)
    tot = jnp.broadcast_to(inc[:, inc.shape[1] - 1 :], inc.shape)
    return pre, tot - inc, tot


def shift_tokens(ids, shifted):
    tok = ids[...]
    count, span = tok.shape
    lane = lax.broadcasted_iota(jnp.int32, tok.shape, 1)
    row = lax.broadcasted_iota(jnp.int32, tok.shape, 0)
    for d in range(-3, 4):
        if d == 0:
            moved = tok
        elif d < 0:
            here = pltpu.roll(tok, -d, axis=1)
            other = jnp.where(row == 0, -1, pltpu.roll(here, 1, axis=0))
            moved = jnp.where(lane < -d, other, here)
        else:
            here = pltpu.roll(tok, span - d, axis=1)
            other = jnp.where(row == count - 1, -1, pltpu.roll(here, count - 1, axis=0))
            moved = jnp.where(lane >= span - d, other, here)
        shifted[d + 3] = moved


def turn_kernel(near_ref, out_ref, turned_ref):
    turned_ref[...] = out_ref[...].T


def states_kernel(
    masks,
    near_ref, far_ref, conv_ref, rate_ref,
    mine_ref, mate_ref, onehot_ref,
    within, total, ids, shifted, x_held, b_held, state,
):
    count = len(masks)
    heads, span = near_ref.shape[1:]
    group, rows, _ = x_held.shape
    width = b_held.shape[1] // 2
    inner = conv_ref.shape[1] - 2 * width
    head = inner // heads
    vocab = conv_ref.shape[2] // 8
    me = lax.axis_index("seq")
    core = me & 1
    base = me - core

    for side, ref in enumerate((near_ref, far_ref)):
        pre, post, tot = unpack(ref[...].reshape(count // 2 * heads, span))
        for slot in range(count // 2):
            c = jnp.bitwise_xor(me, masks[side * (count // 2) + slot])
            block = slice(slot * heads, (slot + 1) * heads)
            within[0, c] = pre[block]
            within[1, c] = post[block]
            total[c] = tot[block]
            ids[pl.ds(c, 1), :] = ref[slot, 0:1] >> 16

    shift_tokens(ids, shifted)
    values = lax.broadcasted_iota(jnp.int32, (vocab, span), 0)

    def onehot(c, sign):
        found = []
        for j in range(4):
            token = shifted[3 + (j - 3) * sign, pl.ds(c, 1), :]
            found.append(jnp.where(values == token, 1.0, 0.0))
        one = jnp.concatenate(found, axis=0).astype(BF16)
        return jnp.concatenate([one, one], axis=0)

    first_head = pl.multiple_of(core * (heads // 2), heads // 2)
    first_row = pl.multiple_of(core * rows, rows)
    some = pl.ds(first_head, heads // 2)

    def remote(i, slot, run):
        rev = i >= base
        b = rev.astype(jnp.int32)
        c = jnp.clip(jnp.where(rev, i + 2, base - 1 - i), 0, count - 1)
        run = jnp.where(i == base, 0.0, run)
        dist = within[1 - b, c, some] + run
        decay = jnp.exp(-rate_ref[b, some] * dist)
        one = onehot(c, 1 - 2 * b)
        x = convolve(conv_ref[b, pl.ds(first_row, rows), :], one)
        x = x.reshape(heads // 2, head, span) * decay[:, None, :]
        x_held[slot] = x.reshape(rows, span).astype(BF16)
        bt = convolve(conv_ref[b, inner : inner + width, :], one)
        ahead = jnp.where(rev, 0.0, bt)
        behind = jnp.where(jnp.logical_and(rev, i < count - 2), bt, 0.0)
        b_held[slot] = jnp.concatenate([ahead, behind], axis=0).astype(BF16)
        return run + total[c, some]

    def gather(g, run, first):
        for k in range(group):
            run = remote(g * group + k, k, run)
        part = jnp.zeros((rows, 2 * width), F32)
        for k in range(group):
            part = part + dot(x_held[k], b_held[k], NT)
        state[...] = part if first else state[...] + part
        return run

    run = gather(0, jnp.zeros((heads // 2, span), F32), True)
    if count - 2 > group:
        lax.fori_loop(1, pl.cdiv(count - 2, group), lambda g, run: gather(g, run, False), run)

    stacked = (heads // 2, head, width)
    through, added = [], []
    for b in range(2):
        c = base + b
        one = onehot(c, 1 - 2 * b)
        decay = jnp.exp(-rate_ref[b, some] * within[1 - b, c, some])
        x = convolve(conv_ref[b, pl.ds(first_row, rows), :], one)
        x = x.reshape(heads // 2, head, span) * decay[:, None, :]
        bt = convolve(conv_ref[b, inner : inner + width, :], one)
        added.append(dot(x.reshape(rows, span).astype(BF16), bt.astype(BF16), NT))
        whole = jnp.exp(-rate_ref[b, some] * total[c, some])
        through.append(whole[:, None, :width])
    ahead, behind = state[:, :width], state[:, width:]
    ahead_next = (ahead.reshape(stacked) * through[0]).reshape(rows, width) + added[0]
    behind_next = (behind.reshape(stacked) * through[1]).reshape(rows, width) + added[1]
    first = jnp.concatenate([ahead, behind_next], axis=1).astype(BF16)
    second = jnp.concatenate([ahead_next, behind], axis=1).astype(BF16)
    mine_ref[...] = jnp.where(core == 0, first, second)
    mate_ref[...] = jnp.where(core == 0, second, first)

    onehot_ref[0] = onehot(me, 1)
    onehot_ref[1] = onehot(me, -1)


def spans_kernel(
    first, masks, held_ref, conv_ref, rate_ref, state_ref, within_ref, total_ref, x_held, b_held
):
    heads, span = held_ref.shape[1:]
    count, inner, width = state_ref.shape
    head = inner // heads
    vocab = conv_ref.shape[2] // 8
    me = lax.axis_index("seq")
    pre, post, tot = unpack(held_ref[first : first + count].reshape(count * heads, span))
    within_ref[0] = pre.reshape(count, heads, span)
    within_ref[1] = post.reshape(count, heads, span)
    total_ref[...] = tot.reshape(count, heads, span)
    lane = lax.broadcasted_iota(jnp.int32, (heads, span), 1)
    values = lax.broadcasted_iota(jnp.int32, (vocab, span), 0)
    for k, mask in enumerate(masks):
        rev = (jnp.bitwise_xor(me, mask) > me) if mask else (me & 1) == 1
        b = rev.astype(jnp.int32)
        token = jnp.broadcast_to(held_ref[first + k, 0:1] >> 16, (vocab, span))
        found = []
        for far in (3, 2, 1, 0):
            there = token
            if far:
                there = jnp.where(rev, pltpu.roll(token, span - far, 1), pltpu.roll(token, far, 1))
            found.append(jnp.where(values == there, 1.0, 0.0))
        one = jnp.concatenate(found, axis=0).astype(BF16)
        one = jnp.concatenate([one, one], axis=0)
        rows = slice(k * heads, (k + 1) * heads)
        decay = jnp.exp(-rate_ref[b] * jnp.where(rev, pre[rows], post[rows]))
        decay = jnp.where(jnp.where(rev, span - 1 - lane, lane) < 3, 0.0, decay)
        x = convolve(conv_ref[b, :inner, :], one).reshape(heads, head, span) * decay[:, None, :]
        bt = convolve(conv_ref[b, inner : inner + width, :], one)
        x_held[k] = x.reshape(inner, span).astype(BF16)
        b_held[k] = bt.astype(BF16)
    for k in range(count):
        for r in range(0, inner, 512):
            state_ref[k, r : r + 512] = dot(x_held[k, r : r + 512], b_held[k], NT)


def combine_kernel(
    masks,
    held_ref, far_ref, state_a, within_a, total_a, state_b, within_b, total_b, conv_ref, rate_ref,
    mine_ref, mate_ref, onehot_ref,
    totals, between, ids, shifted, sums,
):
    count = 2 * len(masks)
    heads, span = held_ref.shape[1:]
    first, inner, width = state_a.shape
    head = inner // heads
    vocab = conv_ref.shape[2] // 8
    me = lax.axis_index("seq")
    core = me & 1
    base = me - core
    parts = [(state_a, within_a, total_a, k) for k in range(first)]
    parts += [(state_b, within_b, total_b, k) for k in range(len(masks) - first)]

    far_e = ((far_ref[...].reshape(len(masks) * heads, span) & 0xFFFF) + 1).astype(F32)
    far_tot = jnp.broadcast_to(jnp.sum(far_e, axis=1, keepdims=True), (len(masks) * heads, LANES))
    for slot, mask in enumerate(masks):
        c = jnp.bitwise_xor(me, mask)
        _, _, tot, k = parts[slot]
        totals[c] = tot[k, :, :LANES]
        ids[pl.ds(c, 1), :] = held_ref[slot, 0:1] >> 16
        c = jnp.bitwise_xor(c, 1)
        totals[c] = far_tot[slot * heads : (slot + 1) * heads]
        ids[pl.ds(c, 1), :] = far_ref[slot, 0:1] >> 16
    run = jnp.zeros((heads, LANES), F32)
    for i in range(count - 2):
        c = jnp.where(i >= base, i + 2, base - 1 - i)
        run = jnp.where(i == base, 0.0, run)
        between[c] = run
        run = run + totals[c]
    between[me] = jnp.zeros((heads, LANES), F32)

    shift_tokens(ids, shifted)
    values = lax.broadcasted_iota(jnp.int32, (vocab, span), 0)
    for b in range(2):
        found = []
        for j in range(4):
            token = shifted[j if b == 0 else 6 - j, pl.ds(me, 1), :]
            found.append(jnp.where(values == token, 1.0, 0.0))
        one = jnp.concatenate(found, axis=0).astype(BF16)
        onehot_ref[b] = jnp.concatenate([one, one], axis=0)

    scales = []
    for slot, mask in enumerate(masks):
        c = jnp.bitwise_xor(me, mask)
        rev = c > me
        scale = jnp.exp(-rate_ref[rev.astype(jnp.int32), :, :LANES] * between[c])
        scales.append((jnp.where(rev, 0.0, scale), jnp.where(rev, scale, 0.0)))
    for h in range(heads):
        rows = slice(h * head, (h + 1) * head)
        ahead = behind = None
        for slot in range(1, len(masks)):
            state, _, _, k = parts[slot]
            value = state[k, rows]
            fore, back = (value * scales[slot][i][h : h + 1] for i in range(2))
            ahead = fore if ahead is None else ahead + fore
            behind = back if behind is None else behind + back
        sums[rows, :width] = ahead
        sums[rows, width:] = behind

    lane = lax.broadcasted_iota(jnp.int32, (1, span), 1)
    token = jnp.full((8, span), -1, jnp.int32)
    kind = jnp.full((1, span), -1, jnp.int32)
    side = jnp.full((1, span), -1, jnp.int32)
    dist = jnp.zeros((heads, LANES), F32)
    rate = jnp.zeros((heads, LANES), F32)
    for slot, mask in enumerate(masks):
        c = jnp.bitwise_xor(me, mask)
        rev = (c > me) if mask else core == 1
        b = rev.astype(jnp.int32)
        here = jnp.logical_and(lane >= 8 * slot, lane < 8 * slot + 3)
        near = here[:, :LANES]
        taps = jnp.concatenate(
            [shifted[3 + (j - 3) * (1 - 2 * b), pl.ds(c, 1), :] for j in (0, 1, 2, 3, 0, 1, 2, 3)],
            axis=0,
        )

        def moved(ahead, behind):
            start = ahead if slot == 0 else pltpu.roll(ahead, 8 * slot, 1)
            return jnp.where(rev, pltpu.roll(behind, 8 * slot + 3, 1), start)

        token = jnp.where(here, moved(taps, taps), token)
        side = jnp.where(here, b, side)
        kind = jnp.where(here, b if mask else 2, kind)
        _, within, _, k = parts[slot]
        gap = moved(within[1, k], within[0, k])[:, :LANES] + between[c]
        dist = jnp.where(near, gap, dist)
        rate = jnp.where(near, rate_ref[b, :, :LANES], rate)
    values = values[:, :LANES]
    found = [jnp.where(values == token[j : j + 1, :LANES], 1.0, 0.0) for j in range(4)]
    one = jnp.concatenate(found, axis=0)
    side, kind = side[:, :LANES], kind[:, :LANES]
    ones = [jnp.where(side == b, one, 0.0).astype(BF16) for b in (0, 0, 1, 1)]
    table = jnp.concatenate(
        [conv_ref[0, : inner + width, :], conv_ref[1, : inner + width, :]], axis=1
    )
    conv = convolve(table, jnp.concatenate(ones, axis=0))
    x = conv[:inner].reshape(heads, head, LANES) * jnp.exp(-rate * dist)[:, None, :]
    bt = conv[inner:]
    bt = jnp.concatenate([jnp.where(kind == i, bt, 0.0) for i in range(3)], axis=0)
    edges = dot(x.reshape(inner, LANES).astype(BF16), bt.astype(BF16), NT)

    through = [jnp.exp(-rate_ref[b, :, :LANES] * totals[base + b]) for b in range(2)]
    zero = core == 0
    for h in range(heads):
        rows = slice(h * head, (h + 1) * head)
        ahead = sums[rows, :width] + edges[rows, :width]
        behind = sums[rows, width:] + edges[rows, width : 2 * width]
        own = edges[rows, 2 * width :] + parts[0][0][0, rows]
        ahead_next = ahead * through[0][h : h + 1]
        behind_next = behind * through[1][h : h + 1]
        mine_ref[rows, :width] = jnp.where(zero, ahead, ahead_next)
        mine_ref[rows, width:] = jnp.where(zero, behind_next, behind)
        mate_ref[rows, :width] = jnp.where(zero, ahead_next + own, ahead).astype(BF16)
        mate_ref[rows, width:] = jnp.where(zero, behind, behind_next + own).astype(BF16)


def own_kernel(
    onehot_ref, conv_ref, decay_ref,
    y_ref, x_ref, scores_ref, c_ref,
):
    inner = y_ref.shape[0]
    width = c_ref.shape[1]
    heads = decay_ref.shape[1]
    head = inner // heads
    for b in range(2):
        conv = convolve(conv_ref[b], onehot_ref[b]).astype(BF16)
        ct = conv[inner + width :]
        c_ref[b] = ct
        scores = dot(conv[inner : inner + width], ct, TN).astype(BF16)
        if b == 1:
            x_ref[...] = conv[:inner]
            scores_ref[...] = scores
            break
        for h in range(heads):
            rows = slice(h * head, (h + 1) * head)
            y_ref[rows] = dot(conv[rows], scores * decay_ref[b, h])


def output_kernel(
    summed,
    mine_ref, mate_ref, reach_ref, decay_ref,
    y_ref, x_ref, scores_ref, c_ref, gates_ref, hgt_ref, out_ref,
    mixed_hbm,
    state, carried, mixin, mixed, sems,
):
    heads, span = reach_ref.shape[1:]
    inner = y_ref.shape[0]
    width = c_ref.shape[1]
    head = inner // heads
    core = lax.axis_index("seq") & 1
    part = inner // 2
    if summed:
        state[...] = (mine_ref[...] + mate_ref[...].astype(F32)).astype(BF16)
    else:
        state[pl.ds(pl.multiple_of(core * part, part), part)] = mine_ref[...]
        state[pl.ds(pl.multiple_of((1 - core) * part, part), part)] = mate_ref[...]
    for b in range(2):
        carried[b] = dot(state[:, b * width : (b + 1) * width], c_ref[b])
    for h in range(heads):
        rows = slice(h * head, (h + 1) * head)
        both = jnp.zeros((head, span), F32)
        for b in range(2):
            if b == 0:
                y = y_ref[rows]
            else:
                y = dot(x_ref[rows], scores_ref[...] * decay_ref[b, h])
            y = y + reach_ref[b, h : h + 1] * carried[b, rows]
            v = y * gates_ref[rows]
            inv = lax.rsqrt(jnp.sum(v * v, axis=0, keepdims=True) * (1.0 / head) + EPS)
            both = both + v * inv * hgt_ref[rows, b : b + 1]
        mixin[rows] = both.astype(BF16)
    columns = mixed.shape[1] // 4
    copies = []
    for k in range(4):
        cols = pl.ds(k * columns, columns)
        mixed[:, cols] = dot(out_ref[cols], mixin[...]).astype(BF16).T
        copies.append(pltpu.make_async_copy(mixed.at[:, cols], mixed_hbm.at[:, cols], sems.at[k]))
        copies[-1].start()
    for copy in copies:
        copy.wait()


def shards(
    ids, exponents, embedding, norm_gain, in_proj, conv_weight, conv_bias, rates, head_gain, out_proj
):
    count = lax.axis_size("seq")
    bits = count.bit_length() - 1
    heads, span = exponents.shape
    vocab = embedding.shape[0]
    inner = out_proj.shape[0]
    wide = conv_bias.shape[1]
    width = (wide - inner) // 2
    taps = conv_weight.shape[1]
    group = min(count - 2, 16)
    pin = lambda value: pltpu.with_memory_space_constraint(value, pltpu.HBM)
    vmem = pl.BlockSpec(memory_space=pltpu.VMEM)
    hbm = pl.BlockSpec(memory_space=pltpu.HBM)
    f32 = lambda *shape: jax.ShapeDtypeStruct(shape, F32)
    b16 = lambda *shape: jax.ShapeDtypeStruct(shape, BF16)

    packed = pl.pallas_call(
        pack_kernel,
        out_shape=jax.ShapeDtypeStruct((1, heads, span), jnp.int32),
        in_specs=[hbm, hbm],
        out_specs=vmem,
        scratch_shapes=[
            pltpu.VMEM((1, span), jnp.int32),
            pltpu.VMEM((heads, span), jnp.int32),
            pltpu.SemaphoreType.DMA((2,)),
        ],
        compiler_params=pltpu.CompilerParams(vmem_limit_bytes=MIB),
        name="pack",
    )(pin(ids[None, :]), pin(exponents))

    def swap(value, mask):
        return lax.ppermute(value, "seq", [(i, i ^ mask) for i in range(count)])

    stages = [[count // 2, count // 2 + count // 4, count // 4]]
    stages += [[1 << bit] for bit in reversed(range(bits - 2))]
    tables = pl.pallas_call(
        prep_kernel,
        out_shape=(
            b16(2, wide, 2 * taps * vocab),
            b16(*embedding.shape),
            f32(inner, LANES),
            f32(2, heads, span),
        ),
        in_specs=[hbm] * 7,
        out_specs=(vmem,) * 4,
        scratch_shapes=[
            pltpu.VMEM((2, heads), F32),
            pltpu.VMEM(embedding.shape, BF16),
            pltpu.VMEM((1, inner), F32),
            pltpu.VMEM((inner, wide), BF16),
            pltpu.VMEM(conv_weight.shape, F32),
            pltpu.VMEM(conv_bias.shape, F32),
            pltpu.VMEM(head_gain.shape, F32),
            pltpu.SemaphoreType.DMA((8,)),
        ],
        compiler_params=pltpu.CompilerParams(vmem_limit_bytes=16 * MIB),
        name="prep",
        cost_estimate=pl.CostEstimate(
            flops=100_000_000, bytes_accessed=12_000_000, transcendentals=2_000_000
        ),
    )(*map(pin, (rates, embedding, norm_gain[None, :], in_proj, conv_weight, conv_bias, head_gain)))

    conv_table, norm_table, gain_table, rate_table = tables
    local = pl.pallas_call(
        local_kernel,
        out_shape=(b16(2, heads, span, span), f32(inner, span), f32(2, heads, span)),
        in_specs=[vmem] * 3 + [hbm],
        out_specs=(vmem,) * 3,
        scratch_shapes=[pltpu.VMEM((inner, inner), BF16), pltpu.SemaphoreType.DMA],
        compiler_params=pltpu.CompilerParams(vmem_limit_bytes=10 * MIB),
        name="local",
        cost_estimate=pl.CostEstimate(
            flops=20_000_000, bytes_accessed=5_000_000, transcendentals=2_000_000
        ),
    )(packed, rate_table, norm_table, pin(in_proj))

    def spans(first, some, held):
        many = len(some)
        return pl.pallas_call(
            functools.partial(spans_kernel, first, some),
            out_shape=(
                f32(many, inner, width), f32(2, many, heads, span), f32(many, heads, span),
            ),
            in_specs=[vmem] * 3,
            out_specs=(vmem,) * 3,
            scratch_shapes=[
                pltpu.VMEM((many, inner, span), BF16), pltpu.VMEM((many, width, span), BF16),
            ],
            compiler_params=pltpu.CompilerParams(vmem_limit_bytes=12 * MIB),
            name="spans",
            cost_estimate=pl.CostEstimate(
                flops=2_000_000_000, bytes_accessed=4_000_000, transcendentals=1_000_000
            ),
        )(held, conv_table, rate_table)

    def turn(value):
        return pl.pallas_call(
            turn_kernel,
            out_shape=b16(*out_proj.shape[::-1]),
            in_specs=[hbm, vmem],
            out_specs=vmem,
            compiler_params=pltpu.CompilerParams(vmem_limit_bytes=4 * MIB),
            name="turn",
            cost_estimate=pl.CostEstimate(
                flops=40_000_000, bytes_accessed=6_000_000, transcendentals=0
            ),
        )(value, out_proj)

    summed = count == 16
    held, masks, early = packed, [0], []
    for k, stage in enumerate(stages[:-1]):
        if k == 1:
            held, local = lax.optimization_barrier((held, local))
        new = [swap(held, mask) for mask in stage]
        if k == 1:
            turned = turn(held)
            if summed:
                early.append(spans(0, masks, held))
        held = jnp.concatenate([held] + new, axis=0)
        masks = masks + [m ^ mask for mask in stage for m in masks]
        if k == 1:
            held, early, turned = lax.optimization_barrier((held, early, turned))
    far = swap(held, 1)
    if summed:
        early.append(spans(len(masks) // 2, masks[len(masks) // 2 :], held))
    decays, gates, reach = local
    if summed:
        mine, mate, onehots = pl.pallas_call(
            functools.partial(combine_kernel, masks),
            out_shape=(f32(inner, 2 * width), b16(inner, 2 * width), b16(2, 2 * taps * vocab, span)),
            in_specs=[vmem] * 10,
            out_specs=(vmem,) * 3,
            scratch_shapes=[
                pltpu.VMEM((count, heads, LANES), F32),
                pltpu.VMEM((count, heads, LANES), F32),
                pltpu.VMEM((count, span), jnp.int32),
                pltpu.VMEM((7, count, span), jnp.int32),
                pltpu.VMEM((inner, 2 * width), F32),
            ],
            compiler_params=pltpu.CompilerParams(vmem_limit_bytes=12 * MIB),
            name="combine",
            cost_estimate=pl.CostEstimate(
                flops=1_000_000_000, bytes_accessed=8_000_000, transcendentals=300_000
            ),
        )(held, far, *early[0], *early[1], conv_table, rate_table)
    else:
        masks = masks + [m ^ 1 for m in masks]
        mine, mate, onehots = pl.pallas_call(
            functools.partial(states_kernel, masks),
            out_shape=(
                b16(inner // 2, 2 * width), b16(inner // 2, 2 * width),
                b16(2, 2 * taps * vocab, span),
            ),
            in_specs=[vmem] * 4,
            out_specs=(vmem,) * 3,
            scratch_shapes=[
                pltpu.VMEM((2, count, heads, span), F32),
                pltpu.VMEM((count, heads, span), F32),
                pltpu.VMEM((count, span), jnp.int32),
                pltpu.VMEM((7, count, span), jnp.int32),
                pltpu.VMEM((group, inner // 2, span), BF16),
                pltpu.VMEM((group, 2 * width, span), BF16),
                pltpu.VMEM((inner // 2, 2 * width), F32),
            ],
            compiler_params=pltpu.CompilerParams(vmem_limit_bytes=(20 if count <= 32 else 32) * MIB),
            name="states",
            cost_estimate=pl.CostEstimate(
                flops=10_000_000_000, bytes_accessed=4_000_000, transcendentals=3_000_000
            ),
        )(held, far, conv_table, rate_table)
    mate = swap(mate, 1)
    own = pl.pallas_call(
        own_kernel,
        out_shape=(
            f32(inner, span), b16(inner, span), b16(span, span),
            b16(2, width, span),
        ),
        in_specs=[vmem] * 3,
        out_specs=(vmem,) * 4,
        compiler_params=pltpu.CompilerParams(vmem_limit_bytes=12 * MIB),
        name="own",
        cost_estimate=pl.CostEstimate(
            flops=3_000_000_000, bytes_accessed=9_000_000, transcendentals=1_000_000
        ),
    )(onehots, conv_table, decays)
    return pl.pallas_call(
        functools.partial(output_kernel, summed),
        out_shape=b16(span, inner),
        in_specs=[vmem] * 11,
        out_specs=hbm,
        scratch_shapes=[
            pltpu.VMEM((inner, 2 * width), BF16),
            pltpu.VMEM((2, inner, span), F32),
            pltpu.VMEM((inner, span), BF16),
            pltpu.VMEM((span, inner), BF16),
            pltpu.SemaphoreType.DMA((4,)),
        ],
        compiler_params=pltpu.CompilerParams(vmem_limit_bytes=14 * MIB),
        name="output",
        cost_estimate=pl.CostEstimate(
            flops=2_000_000_000, bytes_accessed=6_000_000, transcendentals=100_000
        ),
    )(
        mine, mate, reach, decays, *own, gates, gain_table, turned,
    )


def solution(mesh):
    in_specs = (
        P(("parts", "seq")),
        P(None, ("parts", "seq")),
        P(), P(), P(), P(), P(), P(), P(), P(),
    )
    out_specs = P(("parts", "seq"), None)
    return jax.shard_map(shards, mesh=mesh, in_specs=in_specs, out_specs=out_specs, check_vma=False)
```

```python
import functools

import jax
import jax.numpy as jnp
from jax import lax
from jax.experimental import pallas as pl
from jax.experimental.pallas import tpu as pltpu
from jax.sharding import PartitionSpec as P

EPS = 1e-05
LOG2E = 1.4426950408889634
F32 = jnp.float32
BF16 = jnp.bfloat16
NT = (((1,), (1,)), ((), ()))
TN = (((0,), (0,)), ((), ()))
MIB = 1024 * 1024
LANES = 128


def dot(a, b, dims=(((1,), (0,)), ((), ()))):
    return lax.dot_general(a, b, dims, preferred_element_type=F32)


def split(value):
    high = value.astype(BF16)
    return high, (value - high.astype(F32)).astype(BF16)


def sums_before(e):
    span = e.shape[1]
    lower = lax.broadcasted_iota(jnp.int32, (span, span), 0)
    upper = lax.broadcasted_iota(jnp.int32, (span, span), 1)
    before = jnp.where(lower < upper, 1.0, 0.0).astype(BF16)
    high = dot((e >> 8).astype(F32).astype(BF16), before)
    low = dot((e & 255).astype(F32).astype(BF16), before)
    return 256.0 * high + low


def convolve(table, one):
    half = dot(table, one)
    return half + half * jnp.tanh(half)


def pack_kernel(ids_ref, exp_ref, out_ref, ids_buf, exp_buf, sems):
    a = pltpu.make_async_copy(ids_ref, ids_buf, sems.at[0])
    b = pltpu.make_async_copy(exp_ref, exp_buf, sems.at[1])
    a.start()
    b.start()
    a.wait()
    b.wait()
    out_ref[0] = (exp_buf[...] - 1) + (ids_buf[...] << 16)


def prep_kernel(
    rates_hbm, emb_hbm, gain_hbm, in_hbm, cw_hbm, cb_hbm, hg_hbm,
    conv_ref, norm_ref, hgt_ref, rate_ref,
    rates_ref, emb_ref, gain_ref, in_ref, cw_ref, cb_ref, hg_ref, sems,
):
    inner = hg_ref.shape[1]
    taps = cw_ref.shape[1]
    heads, span = rate_ref.shape[1:]
    small = [
        pltpu.make_async_copy(src, dst, sems.at[i])
        for i, (src, dst) in enumerate(
            [
                (rates_hbm, rates_ref), (emb_hbm, emb_ref), (gain_hbm, gain_ref),
                (cw_hbm, cw_ref), (cb_hbm, cb_ref), (hg_hbm, hg_ref),
            ]
        )
    ]
    block = in_ref.shape[1] // 2
    wanted = [
        pltpu.make_async_copy(
            in_hbm.at[:, pl.ds(inner + k * block, block)], in_ref.at[:, pl.ds(k * block, block)],
            sems.at[len(small) + k],
        )
        for k in range(2)
    ]
    for copy in small + wanted:
        copy.start()
    for copy in small:
        copy.wait()
    rates = jnp.concatenate([rates_ref[...], jnp.zeros((6, heads), F32)], axis=0).T
    for b in range(2):
        rate_ref[b] = jnp.broadcast_to(rates[:, b : b + 1], (heads, span))
    hg = jnp.concatenate([hg_ref[...], jnp.zeros((LANES - 2, inner), F32)], axis=0)
    hgt_ref[...] = hg.T
    em = emb_ref[...].astype(F32)
    norm = em * lax.rsqrt(jnp.mean(em * em, axis=1, keepdims=True) + EPS) * gain_ref[...]
    norm = norm.astype(BF16)
    norm_ref[...] = norm
    for k, copy in enumerate(wanted):
        copy.wait()
        cols = slice(k * block, (k + 1) * block)
        proj = dot(norm, in_ref[:, cols]).astype(BF16).astype(F32)
        for b in range(2):
            rows = []
            for j in range(taps):
                row = cw_ref[b, j : j + 1, cols] * proj
                if j == taps - 1:
                    row = row + cb_ref[b : b + 1, cols]
                rows.append(0.5 * row)
            high, low = split(jnp.concatenate(rows, axis=0))
            conv_ref[b, cols] = jnp.concatenate([high, low], axis=0).T


def local_kernel(
    held_ref, rate_ref, norm_ref, in_hbm, decay_ref, gates_ref, reach_ref, in_ref, sem
):
    inner = gates_ref.shape[0]
    fetch = pltpu.make_async_copy(in_hbm.at[:, pl.ds(0, inner)], in_ref, sem)
    fetch.start()
    heads, span = held_ref.shape[1:]
    e = (held_ref[0] & 0xFFFF) + 1
    pre = sums_before(e)
    inc = pre + e.astype(F32)
    half = span // 2
    lower = lax.broadcasted_iota(jnp.int32, (half, half), 0)
    upper = lax.broadcasted_iota(jnp.int32, (half, half), 1)
    zero = jnp.zeros((half, half), BF16)
    for b in range(2):
        cum = inc if b == 0 else pre
        cum_col = cum.T
        keep = lower <= upper if b == 0 else lower >= upper
        factor = rate_ref[b] * (-LOG2E if b == 0 else LOG2E)
        for h in range(heads):
            for p in range(2):
                for q in range(2):
                    rows = slice(p * half, (p + 1) * half)
                    cols = slice(q * half, (q + 1) * half)
                    if (p > q) if b == 0 else (p < q):
                        decay_ref[b, h, rows, cols] = zero
                        continue
                    gap = cum[h : h + 1, cols] - cum_col[rows, h : h + 1]
                    value = jnp.exp2(gap * factor[h : h + 1, :half])
                    if p == q:
                        value = jnp.where(keep, value, 0.0)
                    decay_ref[b, h, rows, cols] = value.astype(BF16)
    reach_ref[0] = jnp.exp(-rate_ref[0] * inc)
    reach_ref[1] = jnp.exp(-rate_ref[1] * (inc[:, span - 1 :] - pre))
    vocab = norm_ref.shape[0]
    values = lax.broadcasted_iota(jnp.int32, (vocab, span), 0)
    current = jnp.where(values == (held_ref[0, 0:1] >> 16), 1.0, 0.0).astype(BF16)
    current = jnp.concatenate([current] * 3 + [jnp.zeros_like(current)], axis=0)
    fetch.wait()
    gate = dot(norm_ref[...], in_ref[...]).astype(BF16).astype(F32)
    gate = gate / (1.0 + jnp.exp(-gate))
    g0 = gate.astype(BF16)
    g1, g2 = split(gate - g0.astype(F32))
    gate = jnp.concatenate([g0, g1, g2, jnp.zeros_like(g0)], axis=0)
    gates_ref[...] = dot(gate, current, TN)


def unpack(raw):
    e = (raw & 0xFFFF) + 1
    pre = sums_before(e)
    inc = pre + e.astype(F32)
    tot = jnp.broadcast_to(inc[:, inc.shape[1] - 1 :], inc.shape)
    return pre, tot - inc, tot


def shift_tokens(ids, shifted):
    tok = ids[...]
    count, span = tok.shape
    lane = lax.broadcasted_iota(jnp.int32, tok.shape, 1)
    row = lax.broadcasted_iota(jnp.int32, tok.shape, 0)
    for d in range(-3, 4):
        if d == 0:
            moved = tok
        elif d < 0:
            here = pltpu.roll(tok, -d, axis=1)
            other = jnp.where(row == 0, -1, pltpu.roll(here, 1, axis=0))
            moved = jnp.where(lane < -d, other, here)
        else:
            here = pltpu.roll(tok, span - d, axis=1)
            other = jnp.where(row == count - 1, -1, pltpu.roll(here, count - 1, axis=0))
            moved = jnp.where(lane >= span - d, other, here)
        shifted[d + 3] = moved


def turn_kernel(near_ref, out_ref, turned_ref):
    turned_ref[...] = out_ref[...].T


def states_kernel(
    masks,
    near_ref, far_ref, conv_ref, rate_ref,
    mine_ref, mate_ref, onehot_ref,
    within, total, ids, shifted, x_held, b_held, state,
):
    count = len(masks)
    heads, span = near_ref.shape[1:]
    group, rows, _ = x_held.shape
    width = b_held.shape[1] // 2
    inner = conv_ref.shape[1] - 2 * width
    head = inner // heads
    vocab = conv_ref.shape[2] // 8
    me = lax.axis_index("seq")
    core = me & 1
    base = me - core

    for side, ref in enumerate((near_ref, far_ref)):
        pre, post, tot = unpack(ref[...].reshape(count // 2 * heads, span))
        for slot in range(count // 2):
            c = jnp.bitwise_xor(me, masks[side * (count // 2) + slot])
            block = slice(slot * heads, (slot + 1) * heads)
            within[0, c] = pre[block]
            within[1, c] = post[block]
            total[c] = tot[block]
            ids[pl.ds(c, 1), :] = ref[slot, 0:1] >> 16

    shift_tokens(ids, shifted)
    values = lax.broadcasted_iota(jnp.int32, (vocab, span), 0)

    def onehot(c, sign):
        found = []
        for j in range(4):
            token = shifted[3 + (j - 3) * sign, pl.ds(c, 1), :]
            found.append(jnp.where(values == token, 1.0, 0.0))
        one = jnp.concatenate(found, axis=0).astype(BF16)
        return jnp.concatenate([one, one], axis=0)

    first_head = pl.multiple_of(core * (heads // 2), heads // 2)
    first_row = pl.multiple_of(core * rows, rows)
    some = pl.ds(first_head, heads // 2)

    def remote(i, slot, run):
        rev = i >= base
        b = rev.astype(jnp.int32)
        c = jnp.clip(jnp.where(rev, i + 2, base - 1 - i), 0, count - 1)
        run = jnp.where(i == base, 0.0, run)
        dist = within[1 - b, c, some] + run
        decay = jnp.exp(-rate_ref[b, some] * dist)
        one = onehot(c, 1 - 2 * b)
        x = convolve(conv_ref[b, pl.ds(first_row, rows), :], one)
        x = x.reshape(heads // 2, head, span) * decay[:, None, :]
        x_held[slot] = x.reshape(rows, span).astype(BF16)
        bt = convolve(conv_ref[b, inner : inner + width, :], one)
        ahead = jnp.where(rev, 0.0, bt)
        behind = jnp.where(jnp.logical_and(rev, i < count - 2), bt, 0.0)
        b_held[slot] = jnp.concatenate([ahead, behind], axis=0).astype(BF16)
        return run + total[c, some]

    def gather(g, run, first):
        for k in range(group):
            run = remote(g * group + k, k, run)
        part = jnp.zeros((rows, 2 * width), F32)
        for k in range(group):
            part = part + dot(x_held[k], b_held[k], NT)
        state[...] = part if first else state[...] + part
        return run

    run = gather(0, jnp.zeros((heads // 2, span), F32), True)
    if count - 2 > group:
        lax.fori_loop(1, pl.cdiv(count - 2, group), lambda g, run: gather(g, run, False), run)

    stacked = (heads // 2, head, width)
    through, added = [], []
    for b in range(2):
        c = base + b
        one = onehot(c, 1 - 2 * b)
        decay = jnp.exp(-rate_ref[b, some] * within[1 - b, c, some])
        x = convolve(conv_ref[b, pl.ds(first_row, rows), :], one)
        x = x.reshape(heads // 2, head, span) * decay[:, None, :]
        bt = convolve(conv_ref[b, inner : inner + width, :], one)
        added.append(dot(x.reshape(rows, span).astype(BF16), bt.astype(BF16), NT))
        whole = jnp.exp(-rate_ref[b, some] * total[c, some])
        through.append(whole[:, None, :width])
    ahead, behind = state[:, :width], state[:, width:]
    ahead_next = (ahead.reshape(stacked) * through[0]).reshape(rows, width) + added[0]
    behind_next = (behind.reshape(stacked) * through[1]).reshape(rows, width) + added[1]
    first = jnp.concatenate([ahead, behind_next], axis=1).astype(BF16)
    second = jnp.concatenate([ahead_next, behind], axis=1).astype(BF16)
    mine_ref[...] = jnp.where(core == 0, first, second)
    mate_ref[...] = jnp.where(core == 0, second, first)

    onehot_ref[0] = onehot(me, 1)
    onehot_ref[1] = onehot(me, -1)


def spans_kernel(
    first, masks, held_ref, conv_ref, rate_ref, state_ref, within_ref, total_ref, x_held, b_held
):
    heads, span = held_ref.shape[1:]
    count, inner, width = state_ref.shape
    head = inner // heads
    vocab = conv_ref.shape[2] // 8
    me = lax.axis_index("seq")
    pre, post, tot = unpack(held_ref[first : first + count].reshape(count * heads, span))
    within_ref[0] = pre.reshape(count, heads, span)
    within_ref[1] = post.reshape(count, heads, span)
    total_ref[...] = tot.reshape(count, heads, span)
    lane = lax.broadcasted_iota(jnp.int32, (heads, span), 1)
    values = lax.broadcasted_iota(jnp.int32, (vocab, span), 0)
    for k, mask in enumerate(masks):
        rev = (jnp.bitwise_xor(me, mask) > me) if mask else (me & 1) == 1
        b = rev.astype(jnp.int32)
        token = jnp.broadcast_to(held_ref[first + k, 0:1] >> 16, (vocab, span))
        found = []
        for far in (3, 2, 1, 0):
            there = token
            if far:
                there = jnp.where(rev, pltpu.roll(token, span - far, 1), pltpu.roll(token, far, 1))
            found.append(jnp.where(values == there, 1.0, 0.0))
        one = jnp.concatenate(found, axis=0).astype(BF16)
        one = jnp.concatenate([one, one], axis=0)
        rows = slice(k * heads, (k + 1) * heads)
        decay = jnp.exp(-rate_ref[b] * jnp.where(rev, pre[rows], post[rows]))
        decay = jnp.where(jnp.where(rev, span - 1 - lane, lane) < 3, 0.0, decay)
        x = convolve(conv_ref[b, :inner, :], one).reshape(heads, head, span) * decay[:, None, :]
        bt = convolve(conv_ref[b, inner : inner + width, :], one)
        x_held[k] = x.reshape(inner, span).astype(BF16)
        b_held[k] = bt.astype(BF16)
    for k in range(count):
        for r in range(0, inner, 512):
            state_ref[k, r : r + 512] = dot(x_held[k, r : r + 512], b_held[k], NT)


def combine_kernel(
    masks,
    held_ref, far_ref, state_a, within_a, total_a, state_b, within_b, total_b, conv_ref, rate_ref,
    mine_ref, mate_ref, onehot_ref,
    totals, between, ids, shifted, sums,
):
    count = 2 * len(masks)
    heads, span = held_ref.shape[1:]
    first, inner, width = state_a.shape
    head = inner // heads
    vocab = conv_ref.shape[2] // 8
    me = lax.axis_index("seq")
    core = me & 1
    base = me - core
    parts = [(state_a, within_a, total_a, k) for k in range(first)]
    parts += [(state_b, within_b, total_b, k) for k in range(len(masks) - first)]

    far_e = ((far_ref[...].reshape(len(masks) * heads, span) & 0xFFFF) + 1).astype(F32)
    far_tot = jnp.broadcast_to(jnp.sum(far_e, axis=1, keepdims=True), (len(masks) * heads, LANES))
    for slot, mask in enumerate(masks):
        c = jnp.bitwise_xor(me, mask)
        _, _, tot, k = parts[slot]
        totals[c] = tot[k, :, :LANES]
        ids[pl.ds(c, 1), :] = held_ref[slot, 0:1] >> 16
        c = jnp.bitwise_xor(c, 1)
        totals[c] = far_tot[slot * heads : (slot + 1) * heads]
        ids[pl.ds(c, 1), :] = far_ref[slot, 0:1] >> 16
    run = jnp.zeros((heads, LANES), F32)
    for i in range(count - 2):
        c = jnp.where(i >= base, i + 2, base - 1 - i)
        run = jnp.where(i == base, 0.0, run)
        between[c] = run
        run = run + totals[c]
    between[me] = jnp.zeros((heads, LANES), F32)

    shift_tokens(ids, shifted)
    values = lax.broadcasted_iota(jnp.int32, (vocab, span), 0)
    for b in range(2):
        found = []
        for j in range(4):
            token = shifted[j if b == 0 else 6 - j, pl.ds(me, 1), :]
            found.append(jnp.where(values == token, 1.0, 0.0))
        one = jnp.concatenate(found, axis=0).astype(BF16)
        onehot_ref[b] = jnp.concatenate([one, one], axis=0)

    scales = []
    for slot, mask in enumerate(masks):
        c = jnp.bitwise_xor(me, mask)
        rev = c > me
        scale = jnp.exp(-rate_ref[rev.astype(jnp.int32), :, :LANES] * between[c])
        scales.append((jnp.where(rev, 0.0, scale), jnp.where(rev, scale, 0.0)))
    for h in range(heads):
        rows = slice(h * head, (h + 1) * head)
        ahead = behind = None
        for slot in range(1, len(masks)):
            state, _, _, k = parts[slot]
            value = state[k, rows]
            fore, back = (value * scales[slot][i][h : h + 1] for i in range(2))
            ahead = fore if ahead is None else ahead + fore
            behind = back if behind is None else behind + back
        sums[rows, :width] = ahead
        sums[rows, width:] = behind

    lane = lax.broadcasted_iota(jnp.int32, (1, span), 1)
    token = jnp.full((8, span), -1, jnp.int32)
    kind = jnp.full((1, span), -1, jnp.int32)
    side = jnp.full((1, span), -1, jnp.int32)
    dist = jnp.zeros((heads, LANES), F32)
    rate = jnp.zeros((heads, LANES), F32)
    for slot, mask in enumerate(masks):
        c = jnp.bitwise_xor(me, mask)
        rev = (c > me) if mask else core == 1
        b = rev.astype(jnp.int32)
        here = jnp.logical_and(lane >= 8 * slot, lane < 8 * slot + 3)
        near = here[:, :LANES]
        taps = jnp.concatenate(
            [shifted[3 + (j - 3) * (1 - 2 * b), pl.ds(c, 1), :] for j in (0, 1, 2, 3, 0, 1, 2, 3)],
            axis=0,
        )

        def moved(ahead, behind):
            start = ahead if slot == 0 else pltpu.roll(ahead, 8 * slot, 1)
            return jnp.where(rev, pltpu.roll(behind, 8 * slot + 3, 1), start)

        token = jnp.where(here, moved(taps, taps), token)
        side = jnp.where(here, b, side)
        kind = jnp.where(here, b if mask else 2, kind)
        _, within, _, k = parts[slot]
        gap = moved(within[1, k], within[0, k])[:, :LANES] + between[c]
        dist = jnp.where(near, gap, dist)
        rate = jnp.where(near, rate_ref[b, :, :LANES], rate)
    values = values[:, :LANES]
    found = [jnp.where(values == token[j : j + 1, :LANES], 1.0, 0.0) for j in range(4)]
    one = jnp.concatenate(found, axis=0)
    side, kind = side[:, :LANES], kind[:, :LANES]
    ones = [jnp.where(side == b, one, 0.0).astype(BF16) for b in (0, 0, 1, 1)]
    table = jnp.concatenate(
        [conv_ref[0, : inner + width, :], conv_ref[1, : inner + width, :]], axis=1
    )
    conv = convolve(table, jnp.concatenate(ones, axis=0))
    x = conv[:inner].reshape(heads, head, LANES) * jnp.exp(-rate * dist)[:, None, :]
    bt = conv[inner:]
    bt = jnp.concatenate([jnp.where(kind == i, bt, 0.0) for i in range(3)], axis=0)
    edges = dot(x.reshape(inner, LANES).astype(BF16), bt.astype(BF16), NT)

    through = [jnp.exp(-rate_ref[b, :, :LANES] * totals[base + b]) for b in range(2)]
    zero = core == 0
    for h in range(heads):
        rows = slice(h * head, (h + 1) * head)
        ahead = sums[rows, :width] + edges[rows, :width]
        behind = sums[rows, width:] + edges[rows, width : 2 * width]
        own = edges[rows, 2 * width :] + parts[0][0][0, rows]
        ahead_next = ahead * through[0][h : h + 1]
        behind_next = behind * through[1][h : h + 1]
        mine_ref[rows, :width] = jnp.where(zero, ahead, ahead_next)
        mine_ref[rows, width:] = jnp.where(zero, behind_next, behind)
        mate_ref[rows, :width] = jnp.where(zero, ahead_next + own, ahead).astype(BF16)
        mate_ref[rows, width:] = jnp.where(zero, behind, behind_next + own).astype(BF16)


def own_kernel(
    onehot_ref, conv_ref, decay_ref,
    y_ref, x_ref, scores_ref, c_ref,
):
    inner = y_ref.shape[0]
    width = c_ref.shape[1]
    heads = decay_ref.shape[1]
    head = inner // heads
    for b in range(2):
        conv = convolve(conv_ref[b], onehot_ref[b]).astype(BF16)
        ct = conv[inner + width :]
        c_ref[b] = ct
        scores = dot(conv[inner : inner + width], ct, TN).astype(BF16)
        if b == 1:
            x_ref[...] = conv[:inner]
            scores_ref[...] = scores
            break
        for h in range(heads):
            rows = slice(h * head, (h + 1) * head)
            y_ref[rows] = dot(conv[rows], scores * decay_ref[b, h])


def output_kernel(
    summed,
    mine_ref, mate_ref, reach_ref, decay_ref,
    y_ref, x_ref, scores_ref, c_ref, gates_ref, hgt_ref, out_ref,
    mixed_hbm,
    state, carried, mixin, mixed, sems,
):
    heads, span = reach_ref.shape[1:]
    inner = y_ref.shape[0]
    width = c_ref.shape[1]
    head = inner // heads
    core = lax.axis_index("seq") & 1
    part = inner // 2
    if summed:
        state[...] = (mine_ref[...] + mate_ref[...].astype(F32)).astype(BF16)
    else:
        state[pl.ds(pl.multiple_of(core * part, part), part)] = mine_ref[...]
        state[pl.ds(pl.multiple_of((1 - core) * part, part), part)] = mate_ref[...]
    for b in range(2):
        carried[b] = dot(state[:, b * width : (b + 1) * width], c_ref[b])
    for h in range(heads):
        rows = slice(h * head, (h + 1) * head)
        both = jnp.zeros((head, span), F32)
        for b in range(2):
            if b == 0:
                y = y_ref[rows]
            else:
                y = dot(x_ref[rows], scores_ref[...] * decay_ref[b, h])
            y = y + reach_ref[b, h : h + 1] * carried[b, rows]
            v = y * gates_ref[rows]
            inv = lax.rsqrt(jnp.sum(v * v, axis=0, keepdims=True) * (1.0 / head) + EPS)
            both = both + v * inv * hgt_ref[rows, b : b + 1]
        mixin[rows] = both.astype(BF16)
    columns = mixed.shape[1] // 4
    copies = []
    for k in range(4):
        cols = pl.ds(k * columns, columns)
        mixed[:, cols] = dot(out_ref[cols], mixin[...]).astype(BF16).T
        copies.append(pltpu.make_async_copy(mixed.at[:, cols], mixed_hbm.at[:, cols], sems.at[k]))
        copies[-1].start()
    for copy in copies:
        copy.wait()


def shards(
    ids, exponents, embedding, norm_gain, in_proj, conv_weight, conv_bias, rates, head_gain, out_proj
):
    count = lax.axis_size("seq")
    bits = count.bit_length() - 1
    heads, span = exponents.shape
    vocab = embedding.shape[0]
    inner = out_proj.shape[0]
    wide = conv_bias.shape[1]
    width = (wide - inner) // 2
    taps = conv_weight.shape[1]
    group = min(count - 2, 16)
    pin = lambda value: pltpu.with_memory_space_constraint(value, pltpu.HBM)
    vmem = pl.BlockSpec(memory_space=pltpu.VMEM)
    hbm = pl.BlockSpec(memory_space=pltpu.HBM)
    f32 = lambda *shape: jax.ShapeDtypeStruct(shape, F32)
    b16 = lambda *shape: jax.ShapeDtypeStruct(shape, BF16)

    packed = pl.pallas_call(
        pack_kernel,
        out_shape=jax.ShapeDtypeStruct((1, heads, span), jnp.int32),
        in_specs=[hbm, hbm],
        out_specs=vmem,
        scratch_shapes=[
            pltpu.VMEM((1, span), jnp.int32),
            pltpu.VMEM((heads, span), jnp.int32),
            pltpu.SemaphoreType.DMA((2,)),
        ],
        compiler_params=pltpu.CompilerParams(vmem_limit_bytes=MIB),
        name="pack",
    )(pin(ids[None, :]), pin(exponents))

    def narrow(value):
        many = value.shape[0]
        low = value & 0xFFFF
        pairs = low[:, : heads // 2] | (low[:, heads // 2 :] << 16)
        token = value[:, 0] >> 16
        token = token[: many // 2] | (token[many // 2 :] << 16)
        token = jnp.pad(token, ((0, heads // 2 - many // 2), (0, 0)))
        return jnp.concatenate([pairs, token[None]], axis=0)

    def widen(value):
        many = value.shape[0] - 1
        pairs, token = value[:many], value[many, : many // 2]
        both = jnp.concatenate([pairs & 0xFFFF, (pairs >> 16) & 0xFFFF], axis=1)
        token = jnp.concatenate([token & 0xFFFF, token >> 16], axis=0)
        return both | (token << 16)[:, None, :]

    def swap(value, mask):
        return lax.ppermute(value, "seq", [(i, i ^ mask) for i in range(count)])

    stages = [[count // 2, count // 2 + count // 4, count // 4]]
    stages += [[1 << bit] for bit in reversed(range(bits - 2))]
    tables = pl.pallas_call(
        prep_kernel,
        out_shape=(
            b16(2, wide, 2 * taps * vocab),
            b16(*embedding.shape),
            f32(inner, LANES),
            f32(2, heads, span),
        ),
        in_specs=[hbm] * 7,
        out_specs=(vmem,) * 4,
        scratch_shapes=[
            pltpu.VMEM((2, heads), F32),
            pltpu.VMEM(embedding.shape, BF16),
            pltpu.VMEM((1, inner), F32),
            pltpu.VMEM((inner, wide), BF16),
            pltpu.VMEM(conv_weight.shape, F32),
            pltpu.VMEM(conv_bias.shape, F32),
            pltpu.VMEM(head_gain.shape, F32),
            pltpu.SemaphoreType.DMA((8,)),
        ],
        compiler_params=pltpu.CompilerParams(vmem_limit_bytes=16 * MIB),
        name="prep",
        cost_estimate=pl.CostEstimate(
            flops=100_000_000, bytes_accessed=12_000_000, transcendentals=2_000_000
        ),
    )(*map(pin, (rates, embedding, norm_gain[None, :], in_proj, conv_weight, conv_bias, head_gain)))

    conv_table, norm_table, gain_table, rate_table = tables
    local = pl.pallas_call(
        local_kernel,
        out_shape=(b16(2, heads, span, span), f32(inner, span), f32(2, heads, span)),
        in_specs=[vmem] * 3 + [hbm],
        out_specs=(vmem,) * 3,
        scratch_shapes=[pltpu.VMEM((inner, inner), BF16), pltpu.SemaphoreType.DMA],
        compiler_params=pltpu.CompilerParams(vmem_limit_bytes=10 * MIB),
        name="local",
        cost_estimate=pl.CostEstimate(
            flops=20_000_000, bytes_accessed=5_000_000, transcendentals=2_000_000
        ),
    )(packed, rate_table, norm_table, pin(in_proj))

    def spans(first, some, held):
        many = len(some)
        return pl.pallas_call(
            functools.partial(spans_kernel, first, some),
            out_shape=(
                f32(many, inner, width), f32(2, many, heads, span), f32(many, heads, span),
            ),
            in_specs=[vmem] * 3,
            out_specs=(vmem,) * 3,
            scratch_shapes=[
                pltpu.VMEM((many, inner, span), BF16), pltpu.VMEM((many, width, span), BF16),
            ],
            compiler_params=pltpu.CompilerParams(vmem_limit_bytes=12 * MIB),
            name="spans",
            cost_estimate=pl.CostEstimate(
                flops=2_000_000_000, bytes_accessed=4_000_000, transcendentals=1_000_000
            ),
        )(held, conv_table, rate_table)

    def turn(value):
        return pl.pallas_call(
            turn_kernel,
            out_shape=b16(*out_proj.shape[::-1]),
            in_specs=[hbm, vmem],
            out_specs=vmem,
            compiler_params=pltpu.CompilerParams(vmem_limit_bytes=4 * MIB),
            name="turn",
            cost_estimate=pl.CostEstimate(
                flops=40_000_000, bytes_accessed=6_000_000, transcendentals=0
            ),
        )(value, out_proj)

    summed = count == 16
    held, masks, early = packed, [0], []
    for k, stage in enumerate(stages[:-1]):
        if k == 1:
            held, local = lax.optimization_barrier((held, local))
        if k == 1 and summed:
            new = [widen(swap(narrow(held), stage[0]))]
        else:
            new = [swap(held, mask) for mask in stage]
        if k == 1:
            turned = turn(held)
            if summed:
                early.append(spans(0, masks, held))
        held = jnp.concatenate([held] + new, axis=0)
        masks = masks + [m ^ mask for mask in stage for m in masks]
        if k == 1:
            held, early, turned = lax.optimization_barrier((held, early, turned))
    far = swap(held, 1)
    if summed:
        early.append(spans(len(masks) // 2, masks[len(masks) // 2 :], held))
    decays, gates, reach = local
    if summed:
        mine, mate, onehots = pl.pallas_call(
            functools.partial(combine_kernel, masks),
            out_shape=(f32(inner, 2 * width), b16(inner, 2 * width), b16(2, 2 * taps * vocab, span)),
            in_specs=[vmem] * 10,
            out_specs=(vmem,) * 3,
            scratch_shapes=[
                pltpu.VMEM((count, heads, LANES), F32),
                pltpu.VMEM((count, heads, LANES), F32),
                pltpu.VMEM((count, span), jnp.int32),
                pltpu.VMEM((7, count, span), jnp.int32),
                pltpu.VMEM((inner, 2 * width), F32),
            ],
            compiler_params=pltpu.CompilerParams(vmem_limit_bytes=12 * MIB),
            name="combine",
            cost_estimate=pl.CostEstimate(
                flops=1_000_000_000, bytes_accessed=8_000_000, transcendentals=300_000
            ),
        )(held, far, *early[0], *early[1], conv_table, rate_table)
    else:
        masks = masks + [m ^ 1 for m in masks]
        mine, mate, onehots = pl.pallas_call(
            functools.partial(states_kernel, masks),
            out_shape=(
                b16(inner // 2, 2 * width), b16(inner // 2, 2 * width),
                b16(2, 2 * taps * vocab, span),
            ),
            in_specs=[vmem] * 4,
            out_specs=(vmem,) * 3,
            scratch_shapes=[
                pltpu.VMEM((2, count, heads, span), F32),
                pltpu.VMEM((count, heads, span), F32),
                pltpu.VMEM((count, span), jnp.int32),
                pltpu.VMEM((7, count, span), jnp.int32),
                pltpu.VMEM((group, inner // 2, span), BF16),
                pltpu.VMEM((group, 2 * width, span), BF16),
                pltpu.VMEM((inner // 2, 2 * width), F32),
            ],
            compiler_params=pltpu.CompilerParams(vmem_limit_bytes=(20 if count <= 32 else 32) * MIB),
            name="states",
            cost_estimate=pl.CostEstimate(
                flops=10_000_000_000, bytes_accessed=4_000_000, transcendentals=3_000_000
            ),
        )(held, far, conv_table, rate_table)
    mate = swap(mate, 1)
    own = pl.pallas_call(
        own_kernel,
        out_shape=(
            f32(inner, span), b16(inner, span), b16(span, span),
            b16(2, width, span),
        ),
        in_specs=[vmem] * 3,
        out_specs=(vmem,) * 4,
        compiler_params=pltpu.CompilerParams(vmem_limit_bytes=12 * MIB),
        name="own",
        cost_estimate=pl.CostEstimate(
            flops=3_000_000_000, bytes_accessed=9_000_000, transcendentals=1_000_000
        ),
    )(onehots, conv_table, decays)
    return pl.pallas_call(
        functools.partial(output_kernel, summed),
        out_shape=b16(span, inner),
        in_specs=[vmem] * 11,
        out_specs=hbm,
        scratch_shapes=[
            pltpu.VMEM((inner, 2 * width), BF16),
            pltpu.VMEM((2, inner, span), F32),
            pltpu.VMEM((inner, span), BF16),
            pltpu.VMEM((span, inner), BF16),
            pltpu.SemaphoreType.DMA((4,)),
        ],
        compiler_params=pltpu.CompilerParams(vmem_limit_bytes=14 * MIB),
        name="output",
        cost_estimate=pl.CostEstimate(
            flops=2_000_000_000, bytes_accessed=6_000_000, transcendentals=100_000
        ),
    )(
        mine, mate, reach, decays, *own, gates, gain_table, turned,
    )


def solution(mesh):
    in_specs = (
        P(("parts", "seq")),
        P(None, ("parts", "seq")),
        P(), P(), P(), P(), P(), P(), P(), P(),
    )
    out_specs = P(("parts", "seq"), None)
    return jax.shard_map(shards, mesh=mesh, in_specs=in_specs, out_specs=out_specs, check_vma=False)
```

```python
import functools

import jax
import jax.numpy as jnp
from jax import lax
from jax.experimental import pallas as pl
from jax.experimental.pallas import tpu as pltpu
from jax.sharding import PartitionSpec as P

EPS = 1e-05
LOG2E = 1.4426950408889634
F32 = jnp.float32
BF16 = jnp.bfloat16
NT = (((1,), (1,)), ((), ()))
TN = (((0,), (0,)), ((), ()))
MIB = 1024 * 1024
LANES = 128


def dot(a, b, dims=(((1,), (0,)), ((), ()))):
    return lax.dot_general(a, b, dims, preferred_element_type=F32)


def split(value):
    high = value.astype(BF16)
    return high, (value - high.astype(F32)).astype(BF16)


def sums_before(e):
    span = e.shape[1]
    lower = lax.broadcasted_iota(jnp.int32, (span, span), 0)
    upper = lax.broadcasted_iota(jnp.int32, (span, span), 1)
    before = jnp.where(lower < upper, 1.0, 0.0).astype(BF16)
    high = dot((e >> 8).astype(F32).astype(BF16), before)
    low = dot((e & 255).astype(F32).astype(BF16), before)
    return 256.0 * high + low


def convolve(table, one):
    half = dot(table, one)
    return half + half * jnp.tanh(half)


def pack_kernel(ids_ref, exp_ref, out_ref, ids_buf, exp_buf, sems):
    a = pltpu.make_async_copy(ids_ref, ids_buf, sems.at[0])
    b = pltpu.make_async_copy(exp_ref, exp_buf, sems.at[1])
    a.start()
    b.start()
    a.wait()
    b.wait()
    out_ref[0] = (exp_buf[...] - 1) + (ids_buf[...] << 16)


def prep_kernel(
    rates_hbm, emb_hbm, gain_hbm, in_hbm, cw_hbm, cb_hbm, hg_hbm,
    conv_ref, norm_ref, hgt_ref, rate_ref,
    rates_ref, emb_ref, gain_ref, in_ref, cw_ref, cb_ref, hg_ref, sems,
):
    inner = hg_ref.shape[1]
    taps = cw_ref.shape[1]
    heads, span = rate_ref.shape[1:]
    small = [
        pltpu.make_async_copy(src, dst, sems.at[i])
        for i, (src, dst) in enumerate(
            [
                (rates_hbm, rates_ref), (emb_hbm, emb_ref), (gain_hbm, gain_ref),
                (cw_hbm, cw_ref), (cb_hbm, cb_ref), (hg_hbm, hg_ref),
            ]
        )
    ]
    block = in_ref.shape[1] // 2
    wanted = [
        pltpu.make_async_copy(
            in_hbm.at[:, pl.ds(inner + k * block, block)], in_ref.at[:, pl.ds(k * block, block)],
            sems.at[len(small) + k],
        )
        for k in range(2)
    ]
    for copy in small + wanted:
        copy.start()
    for copy in small:
        copy.wait()
    rates = jnp.concatenate([rates_ref[...], jnp.zeros((6, heads), F32)], axis=0).T
    for b in range(2):
        rate_ref[b] = jnp.broadcast_to(rates[:, b : b + 1], (heads, span))
    hg = jnp.concatenate([hg_ref[...], jnp.zeros((LANES - 2, inner), F32)], axis=0)
    hgt_ref[...] = hg.T
    em = emb_ref[...].astype(F32)
    norm = em * lax.rsqrt(jnp.mean(em * em, axis=1, keepdims=True) + EPS) * gain_ref[...]
    norm = norm.astype(BF16)
    norm_ref[...] = norm
    for k, copy in enumerate(wanted):
        copy.wait()
        cols = slice(k * block, (k + 1) * block)
        proj = dot(norm, in_ref[:, cols]).astype(BF16).astype(F32)
        for b in range(2):
            rows = []
            for j in range(taps):
                row = cw_ref[b, j : j + 1, cols] * proj
                if j == taps - 1:
                    row = row + cb_ref[b : b + 1, cols]
                rows.append(0.5 * row)
            high, low = split(jnp.concatenate(rows, axis=0))
            conv_ref[b, cols] = jnp.concatenate([high, low], axis=0).T


def local_kernel(
    held_ref, rate_ref, norm_ref, in_hbm, decay_ref, gates_ref, reach_ref, in_ref, sem
):
    inner = gates_ref.shape[0]
    fetch = pltpu.make_async_copy(in_hbm.at[:, pl.ds(0, inner)], in_ref, sem)
    fetch.start()
    heads, span = held_ref.shape[1:]
    e = (held_ref[0] & 0xFFFF) + 1
    pre = sums_before(e)
    inc = pre + e.astype(F32)
    half = span // 2
    lower = lax.broadcasted_iota(jnp.int32, (half, half), 0)
    upper = lax.broadcasted_iota(jnp.int32, (half, half), 1)
    zero = jnp.zeros((half, half), BF16)
    for b in range(2):
        cum = inc if b == 0 else pre
        cum_col = cum.T
        keep = lower <= upper if b == 0 else lower >= upper
        factor = rate_ref[b] * (-LOG2E if b == 0 else LOG2E)
        for h in range(heads):
            for p in range(2):
                for q in range(2):
                    rows = slice(p * half, (p + 1) * half)
                    cols = slice(q * half, (q + 1) * half)
                    if (p > q) if b == 0 else (p < q):
                        decay_ref[b, h, rows, cols] = zero
                        continue
                    gap = cum[h : h + 1, cols] - cum_col[rows, h : h + 1]
                    value = jnp.exp2(gap * factor[h : h + 1, :half])
                    if p == q:
                        value = jnp.where(keep, value, 0.0)
                    decay_ref[b, h, rows, cols] = value.astype(BF16)
    reach_ref[0] = jnp.exp(-rate_ref[0] * inc)
    reach_ref[1] = jnp.exp(-rate_ref[1] * (inc[:, span - 1 :] - pre))
    vocab = norm_ref.shape[0]
    values = lax.broadcasted_iota(jnp.int32, (vocab, span), 0)
    current = jnp.where(values == (held_ref[0, 0:1] >> 16), 1.0, 0.0).astype(BF16)
    current = jnp.concatenate([current] * 3 + [jnp.zeros_like(current)], axis=0)
    fetch.wait()
    gate = dot(norm_ref[...], in_ref[...]).astype(BF16).astype(F32)
    gate = gate / (1.0 + jnp.exp(-gate))
    g0 = gate.astype(BF16)
    g1, g2 = split(gate - g0.astype(F32))
    gate = jnp.concatenate([g0, g1, g2, jnp.zeros_like(g0)], axis=0)
    gates_ref[...] = dot(gate, current, TN)


def unpack(raw):
    e = (raw & 0xFFFF) + 1
    pre = sums_before(e)
    inc = pre + e.astype(F32)
    tot = jnp.broadcast_to(inc[:, inc.shape[1] - 1 :], inc.shape)
    return pre, tot - inc, tot


def shift_tokens(ids, shifted):
    tok = ids[...]
    count, span = tok.shape
    lane = lax.broadcasted_iota(jnp.int32, tok.shape, 1)
    row = lax.broadcasted_iota(jnp.int32, tok.shape, 0)
    for d in range(-3, 4):
        if d == 0:
            moved = tok
        elif d < 0:
            here = pltpu.roll(tok, -d, axis=1)
            other = jnp.where(row == 0, -1, pltpu.roll(here, 1, axis=0))
            moved = jnp.where(lane < -d, other, here)
        else:
            here = pltpu.roll(tok, span - d, axis=1)
            other = jnp.where(row == count - 1, -1, pltpu.roll(here, count - 1, axis=0))
            moved = jnp.where(lane >= span - d, other, here)
        shifted[d + 3] = moved


def turn_kernel(near_ref, out_ref, turned_ref):
    turned_ref[...] = out_ref[...].T


def states_kernel(
    masks,
    near_ref, far_ref, conv_ref, rate_ref,
    mine_ref, mate_ref, onehot_ref,
    within, total, ids, shifted, x_held, b_held, state,
):
    count = len(masks)
    heads, span = near_ref.shape[1:]
    group, rows, _ = x_held.shape
    width = b_held.shape[1] // 2
    inner = conv_ref.shape[1] - 2 * width
    head = inner // heads
    vocab = conv_ref.shape[2] // 8
    me = lax.axis_index("seq")
    core = me & 1
    base = me - core

    for side, ref in enumerate((near_ref, far_ref)):
        pre, post, tot = unpack(ref[...].reshape(count // 2 * heads, span))
        for slot in range(count // 2):
            c = jnp.bitwise_xor(me, masks[side * (count // 2) + slot])
            block = slice(slot * heads, (slot + 1) * heads)
            within[0, c] = pre[block]
            within[1, c] = post[block]
            total[c] = tot[block]
            ids[pl.ds(c, 1), :] = ref[slot, 0:1] >> 16

    shift_tokens(ids, shifted)
    values = lax.broadcasted_iota(jnp.int32, (vocab, span), 0)

    def onehot(c, sign):
        found = []
        for j in range(4):
            token = shifted[3 + (j - 3) * sign, pl.ds(c, 1), :]
            found.append(jnp.where(values == token, 1.0, 0.0))
        one = jnp.concatenate(found, axis=0).astype(BF16)
        return jnp.concatenate([one, one], axis=0)

    first_head = pl.multiple_of(core * (heads // 2), heads // 2)
    first_row = pl.multiple_of(core * rows, rows)
    some = pl.ds(first_head, heads // 2)

    def remote(i, slot, run):
        rev = i >= base
        b = rev.astype(jnp.int32)
        c = jnp.clip(jnp.where(rev, i + 2, base - 1 - i), 0, count - 1)
        run = jnp.where(i == base, 0.0, run)
        dist = within[1 - b, c, some] + run
        decay = jnp.exp(-rate_ref[b, some] * dist)
        one = onehot(c, 1 - 2 * b)
        x = convolve(conv_ref[b, pl.ds(first_row, rows), :], one)
        x = x.reshape(heads // 2, head, span) * decay[:, None, :]
        x_held[slot] = x.reshape(rows, span).astype(BF16)
        bt = convolve(conv_ref[b, inner : inner + width, :], one)
        ahead = jnp.where(rev, 0.0, bt)
        behind = jnp.where(jnp.logical_and(rev, i < count - 2), bt, 0.0)
        b_held[slot] = jnp.concatenate([ahead, behind], axis=0).astype(BF16)
        return run + total[c, some]

    def gather(g, run, first):
        for k in range(group):
            run = remote(g * group + k, k, run)
        part = jnp.zeros((rows, 2 * width), F32)
        for k in range(group):
            part = part + dot(x_held[k], b_held[k], NT)
        state[...] = part if first else state[...] + part
        return run

    run = gather(0, jnp.zeros((heads // 2, span), F32), True)
    if count - 2 > group:
        lax.fori_loop(1, pl.cdiv(count - 2, group), lambda g, run: gather(g, run, False), run)

    stacked = (heads // 2, head, width)
    through, added = [], []
    for b in range(2):
        c = base + b
        one = onehot(c, 1 - 2 * b)
        decay = jnp.exp(-rate_ref[b, some] * within[1 - b, c, some])
        x = convolve(conv_ref[b, pl.ds(first_row, rows), :], one)
        x = x.reshape(heads // 2, head, span) * decay[:, None, :]
        bt = convolve(conv_ref[b, inner : inner + width, :], one)
        added.append(dot(x.reshape(rows, span).astype(BF16), bt.astype(BF16), NT))
        whole = jnp.exp(-rate_ref[b, some] * total[c, some])
        through.append(whole[:, None, :width])
    ahead, behind = state[:, :width], state[:, width:]
    ahead_next = (ahead.reshape(stacked) * through[0]).reshape(rows, width) + added[0]
    behind_next = (behind.reshape(stacked) * through[1]).reshape(rows, width) + added[1]
    first = jnp.concatenate([ahead, behind_next], axis=1).astype(BF16)
    second = jnp.concatenate([ahead_next, behind], axis=1).astype(BF16)
    mine_ref[...] = jnp.where(core == 0, first, second)
    mate_ref[...] = jnp.where(core == 0, second, first)

    onehot_ref[0] = onehot(me, 1)
    onehot_ref[1] = onehot(me, -1)


def spans_kernel(
    first, masks, held_ref, conv_ref, rate_ref, state_ref, within_ref, total_ref, x_held, b_held
):
    heads, span = held_ref.shape[1:]
    count, inner, width = state_ref.shape
    head = inner // heads
    vocab = conv_ref.shape[2] // 8
    me = lax.axis_index("seq")
    pre, post, tot = unpack(held_ref[first : first + count].reshape(count * heads, span))
    within_ref[0] = pre.reshape(count, heads, span)
    within_ref[1] = post.reshape(count, heads, span)
    total_ref[...] = tot.reshape(count, heads, span)
    lane = lax.broadcasted_iota(jnp.int32, (heads, span), 1)
    values = lax.broadcasted_iota(jnp.int32, (vocab, span), 0)
    for k, mask in enumerate(masks):
        rev = (jnp.bitwise_xor(me, mask) > me) if mask else (me & 1) == 1
        b = rev.astype(jnp.int32)
        token = jnp.broadcast_to(held_ref[first + k, 0:1] >> 16, (vocab, span))
        found = []
        for far in (3, 2, 1, 0):
            there = token
            if far:
                there = jnp.where(rev, pltpu.roll(token, span - far, 1), pltpu.roll(token, far, 1))
            found.append(jnp.where(values == there, 1.0, 0.0))
        one = jnp.concatenate(found, axis=0).astype(BF16)
        one = jnp.concatenate([one, one], axis=0)
        rows = slice(k * heads, (k + 1) * heads)
        decay = jnp.exp(-rate_ref[b] * jnp.where(rev, pre[rows], post[rows]))
        decay = jnp.where(jnp.where(rev, span - 1 - lane, lane) < 3, 0.0, decay)
        x = convolve(conv_ref[b, :inner, :], one).reshape(heads, head, span) * decay[:, None, :]
        bt = convolve(conv_ref[b, inner : inner + width, :], one)
        x_held[k] = x.reshape(inner, span).astype(BF16)
        b_held[k] = bt.astype(BF16)
    for k in range(count):
        for r in range(0, inner, 512):
            state_ref[k, r : r + 512] = dot(x_held[k, r : r + 512], b_held[k], NT)


def combine_kernel(
    masks,
    held_ref, far_ref, state_a, within_a, total_a, state_b, within_b, total_b, conv_ref, rate_ref,
    mine_ref, mate_ref, onehot_ref,
    totals, between, ids, shifted, sums,
):
    count = 2 * len(masks)
    heads, span = held_ref.shape[1:]
    first, inner, width = state_a.shape
    head = inner // heads
    vocab = conv_ref.shape[2] // 8
    me = lax.axis_index("seq")
    core = me & 1
    base = me - core
    parts = [(state_a, within_a, total_a, k) for k in range(first)]
    parts += [(state_b, within_b, total_b, k) for k in range(len(masks) - first)]

    far_e = ((far_ref[...].reshape(len(masks) * heads, span) & 0xFFFF) + 1).astype(F32)
    far_tot = jnp.broadcast_to(jnp.sum(far_e, axis=1, keepdims=True), (len(masks) * heads, LANES))
    for slot, mask in enumerate(masks):
        c = jnp.bitwise_xor(me, mask)
        _, _, tot, k = parts[slot]
        totals[c] = tot[k, :, :LANES]
        ids[pl.ds(c, 1), :] = held_ref[slot, 0:1] >> 16
        c = jnp.bitwise_xor(c, 1)
        totals[c] = far_tot[slot * heads : (slot + 1) * heads]
        ids[pl.ds(c, 1), :] = far_ref[slot, 0:1] >> 16
    run = jnp.zeros((heads, LANES), F32)
    for i in range(count - 2):
        c = jnp.where(i >= base, i + 2, base - 1 - i)
        run = jnp.where(i == base, 0.0, run)
        between[c] = run
        run = run + totals[c]
    between[me] = jnp.zeros((heads, LANES), F32)

    shift_tokens(ids, shifted)
    values = lax.broadcasted_iota(jnp.int32, (vocab, span), 0)
    for b in range(2):
        found = []
        for j in range(4):
            token = shifted[j if b == 0 else 6 - j, pl.ds(me, 1), :]
            found.append(jnp.where(values == token, 1.0, 0.0))
        one = jnp.concatenate(found, axis=0).astype(BF16)
        onehot_ref[b] = jnp.concatenate([one, one], axis=0)

    scales = []
    for slot, mask in enumerate(masks):
        c = jnp.bitwise_xor(me, mask)
        rev = c > me
        scale = jnp.exp(-rate_ref[rev.astype(jnp.int32), :, :LANES] * between[c])
        scales.append(scale)
    for h in range(heads):
        rows = slice(h * head, (h + 1) * head)
        groups = {}
        for slot in range(1, len(masks)):
            state, _, _, k = parts[slot]
            value = state[k, rows] * scales[slot][h : h + 1]
            top = 1 << (masks[slot].bit_length() - 1)
            groups[top] = groups[top] + value if top in groups else value
        ahead = behind = 0.0
        for top, value in groups.items():
            rev = (me & top) == 0
            ahead = ahead + jnp.where(rev, 0.0, value)
            behind = behind + jnp.where(rev, value, 0.0)
        sums[rows, :width] = ahead
        sums[rows, width:] = behind

    lane = lax.broadcasted_iota(jnp.int32, (1, span), 1)
    token = jnp.full((8, span), -1, jnp.int32)
    kind = jnp.full((1, span), -1, jnp.int32)
    side = jnp.full((1, span), -1, jnp.int32)
    dist = jnp.zeros((heads, LANES), F32)
    rate = jnp.zeros((heads, LANES), F32)
    for slot, mask in enumerate(masks):
        c = jnp.bitwise_xor(me, mask)
        rev = (c > me) if mask else core == 1
        b = rev.astype(jnp.int32)
        here = jnp.logical_and(lane >= 8 * slot, lane < 8 * slot + 3)
        near = here[:, :LANES]
        taps = jnp.concatenate(
            [shifted[3 + (j - 3) * (1 - 2 * b), pl.ds(c, 1), :] for j in (0, 1, 2, 3, 0, 1, 2, 3)],
            axis=0,
        )

        def moved(ahead, behind):
            start = ahead if slot == 0 else pltpu.roll(ahead, 8 * slot, 1)
            return jnp.where(rev, pltpu.roll(behind, 8 * slot + 3, 1), start)

        token = jnp.where(here, moved(taps, taps), token)
        side = jnp.where(here, b, side)
        kind = jnp.where(here, b if mask else 2, kind)
        _, within, _, k = parts[slot]
        gap = moved(within[1, k], within[0, k])[:, :LANES] + between[c]
        dist = jnp.where(near, gap, dist)
        rate = jnp.where(near, rate_ref[b, :, :LANES], rate)
    values = values[:, :LANES]
    found = [jnp.where(values == token[j : j + 1, :LANES], 1.0, 0.0) for j in range(4)]
    one = jnp.concatenate(found, axis=0)
    side, kind = side[:, :LANES], kind[:, :LANES]
    ones = [jnp.where(side == b, one, 0.0).astype(BF16) for b in (0, 0, 1, 1)]
    table = jnp.concatenate(
        [conv_ref[0, : inner + width, :], conv_ref[1, : inner + width, :]], axis=1
    )
    conv = convolve(table, jnp.concatenate(ones, axis=0))
    x = conv[:inner].reshape(heads, head, LANES) * jnp.exp(-rate * dist)[:, None, :]
    bt = conv[inner:]
    bt = jnp.concatenate([jnp.where(kind == i, bt, 0.0) for i in range(3)], axis=0)
    edges = dot(x.reshape(inner, LANES).astype(BF16), bt.astype(BF16), NT)

    through = [jnp.exp(-rate_ref[b, :, :LANES] * totals[base + b]) for b in range(2)]
    zero = core == 0
    for h in range(heads):
        rows = slice(h * head, (h + 1) * head)
        ahead = sums[rows, :width] + edges[rows, :width]
        behind = sums[rows, width:] + edges[rows, width : 2 * width]
        own = edges[rows, 2 * width :] + parts[0][0][0, rows]
        ahead_next = ahead * through[0][h : h + 1]
        behind_next = behind * through[1][h : h + 1]
        mine_ref[rows, :width] = jnp.where(zero, ahead, ahead_next)
        mine_ref[rows, width:] = jnp.where(zero, behind_next, behind)
        mate_ref[rows, :width] = jnp.where(zero, ahead_next + own, ahead).astype(BF16)
        mate_ref[rows, width:] = jnp.where(zero, behind, behind_next + own).astype(BF16)


def own_kernel(
    onehot_ref, conv_ref, decay_ref,
    y_ref, x_ref, scores_ref, c_ref,
):
    inner = y_ref.shape[0]
    width = c_ref.shape[1]
    heads = decay_ref.shape[1]
    head = inner // heads
    for b in range(2):
        conv = convolve(conv_ref[b], onehot_ref[b]).astype(BF16)
        ct = conv[inner + width :]
        c_ref[b] = ct
        scores = dot(conv[inner : inner + width], ct, TN).astype(BF16)
        if b == 1:
            x_ref[...] = conv[:inner]
            scores_ref[...] = scores
            break
        for h in range(heads):
            rows = slice(h * head, (h + 1) * head)
            y_ref[rows] = dot(conv[rows], scores * decay_ref[b, h])


def output_kernel(
    summed,
    mine_ref, mate_ref, reach_ref, decay_ref,
    y_ref, x_ref, scores_ref, c_ref, gates_ref, hgt_ref, out_ref,
    mixed_hbm,
    state, carried, mixin, mixed, sems,
):
    heads, span = reach_ref.shape[1:]
    inner = y_ref.shape[0]
    width = c_ref.shape[1]
    head = inner // heads
    core = lax.axis_index("seq") & 1
    part = inner // 2
    if summed:
        state[...] = (mine_ref[...] + mate_ref[...].astype(F32)).astype(BF16)
    else:
        state[pl.ds(pl.multiple_of(core * part, part), part)] = mine_ref[...]
        state[pl.ds(pl.multiple_of((1 - core) * part, part), part)] = mate_ref[...]
    for b in range(2):
        carried[b] = dot(state[:, b * width : (b + 1) * width], c_ref[b])
    for h in range(heads):
        rows = slice(h * head, (h + 1) * head)
        both = jnp.zeros((head, span), F32)
        for b in range(2):
            if b == 0:
                y = y_ref[rows]
            else:
                y = dot(x_ref[rows], scores_ref[...] * decay_ref[b, h])
            y = y + reach_ref[b, h : h + 1] * carried[b, rows]
            v = y * gates_ref[rows]
            inv = lax.rsqrt(jnp.sum(v * v, axis=0, keepdims=True) * (1.0 / head) + EPS)
            both = both + v * inv * hgt_ref[rows, b : b + 1]
        mixin[rows] = both.astype(BF16)
    columns = mixed.shape[1] // 4
    copies = []
    for k in range(4):
        cols = pl.ds(k * columns, columns)
        mixed[:, cols] = dot(out_ref[cols], mixin[...]).astype(BF16).T
        copies.append(pltpu.make_async_copy(mixed.at[:, cols], mixed_hbm.at[:, cols], sems.at[k]))
        copies[-1].start()
    for copy in copies:
        copy.wait()


def shards(
    ids, exponents, embedding, norm_gain, in_proj, conv_weight, conv_bias, rates, head_gain, out_proj
):
    count = lax.axis_size("seq")
    bits = count.bit_length() - 1
    heads, span = exponents.shape
    vocab = embedding.shape[0]
    inner = out_proj.shape[0]
    wide = conv_bias.shape[1]
    width = (wide - inner) // 2
    taps = conv_weight.shape[1]
    group = min(count - 2, 16)
    pin = lambda value: pltpu.with_memory_space_constraint(value, pltpu.HBM)
    vmem = pl.BlockSpec(memory_space=pltpu.VMEM)
    hbm = pl.BlockSpec(memory_space=pltpu.HBM)
    f32 = lambda *shape: jax.ShapeDtypeStruct(shape, F32)
    b16 = lambda *shape: jax.ShapeDtypeStruct(shape, BF16)

    packed = pl.pallas_call(
        pack_kernel,
        out_shape=jax.ShapeDtypeStruct((1, heads, span), jnp.int32),
        in_specs=[hbm, hbm],
        out_specs=vmem,
        scratch_shapes=[
            pltpu.VMEM((1, span), jnp.int32),
            pltpu.VMEM((heads, span), jnp.int32),
            pltpu.SemaphoreType.DMA((2,)),
        ],
        compiler_params=pltpu.CompilerParams(vmem_limit_bytes=MIB),
        name="pack",
    )(pin(ids[None, :]), pin(exponents))

    def narrow(value):
        many = value.shape[0]
        low = value & 0xFFFF
        pairs = low[:, : heads // 2] | (low[:, heads // 2 :] << 16)
        token = value[:, 0] >> 16
        token = token[: many // 2] | (token[many // 2 :] << 16)
        token = jnp.pad(token, ((0, heads // 2 - many // 2), (0, 0)))
        return jnp.concatenate([pairs, token[None]], axis=0)

    def widen(value):
        many = value.shape[0] - 1
        pairs, token = value[:many], value[many, : many // 2]
        both = jnp.concatenate([pairs & 0xFFFF, (pairs >> 16) & 0xFFFF], axis=1)
        token = jnp.concatenate([token & 0xFFFF, token >> 16], axis=0)
        return both | (token << 16)[:, None, :]

    def swap(value, mask):
        return lax.ppermute(value, "seq", [(i, i ^ mask) for i in range(count)])

    stages = [[count // 2, count // 2 + count // 4, count // 4]]
    stages += [[1 << bit] for bit in reversed(range(bits - 2))]
    tables = pl.pallas_call(
        prep_kernel,
        out_shape=(
            b16(2, wide, 2 * taps * vocab),
            b16(*embedding.shape),
            f32(inner, LANES),
            f32(2, heads, span),
        ),
        in_specs=[hbm] * 7,
        out_specs=(vmem,) * 4,
        scratch_shapes=[
            pltpu.VMEM((2, heads), F32),
            pltpu.VMEM(embedding.shape, BF16),
            pltpu.VMEM((1, inner), F32),
            pltpu.VMEM((inner, wide), BF16),
            pltpu.VMEM(conv_weight.shape, F32),
            pltpu.VMEM(conv_bias.shape, F32),
            pltpu.VMEM(head_gain.shape, F32),
            pltpu.SemaphoreType.DMA((8,)),
        ],
        compiler_params=pltpu.CompilerParams(vmem_limit_bytes=16 * MIB),
        name="prep",
        cost_estimate=pl.CostEstimate(
            flops=100_000_000, bytes_accessed=12_000_000, transcendentals=2_000_000
        ),
    )(*map(pin, (rates, embedding, norm_gain[None, :], in_proj, conv_weight, conv_bias, head_gain)))

    conv_table, norm_table, gain_table, rate_table = tables
    local = pl.pallas_call(
        local_kernel,
        out_shape=(b16(2, heads, span, span), f32(inner, span), f32(2, heads, span)),
        in_specs=[vmem] * 3 + [hbm],
        out_specs=(vmem,) * 3,
        scratch_shapes=[pltpu.VMEM((inner, inner), BF16), pltpu.SemaphoreType.DMA],
        compiler_params=pltpu.CompilerParams(vmem_limit_bytes=10 * MIB),
        name="local",
        cost_estimate=pl.CostEstimate(
            flops=20_000_000, bytes_accessed=5_000_000, transcendentals=2_000_000
        ),
    )(packed, rate_table, norm_table, pin(in_proj))

    def spans(first, some, held):
        many = len(some)
        return pl.pallas_call(
            functools.partial(spans_kernel, first, some),
            out_shape=(
                f32(many, inner, width), f32(2, many, heads, span), f32(many, heads, span),
            ),
            in_specs=[vmem] * 3,
            out_specs=(vmem,) * 3,
            scratch_shapes=[
                pltpu.VMEM((many, inner, span), BF16), pltpu.VMEM((many, width, span), BF16),
            ],
            compiler_params=pltpu.CompilerParams(vmem_limit_bytes=12 * MIB),
            name="spans",
            cost_estimate=pl.CostEstimate(
                flops=2_000_000_000, bytes_accessed=4_000_000, transcendentals=1_000_000
            ),
        )(held, conv_table, rate_table)

    def turn(value):
        return pl.pallas_call(
            turn_kernel,
            out_shape=b16(*out_proj.shape[::-1]),
            in_specs=[hbm, vmem],
            out_specs=vmem,
            compiler_params=pltpu.CompilerParams(vmem_limit_bytes=4 * MIB),
            name="turn",
            cost_estimate=pl.CostEstimate(
                flops=40_000_000, bytes_accessed=6_000_000, transcendentals=0
            ),
        )(value, out_proj)

    summed = count == 16
    held, masks, early = packed, [0], []
    for k, stage in enumerate(stages[:-1]):
        if k == 1:
            held, local = lax.optimization_barrier((held, local))
        if k == 1 and summed:
            new = [widen(swap(narrow(held), stage[0]))]
        else:
            new = [swap(held, mask) for mask in stage]
        if k == 1:
            turned = turn(held)
            if summed:
                early.append(spans(0, masks, held))
        held = jnp.concatenate([held] + new, axis=0)
        masks = masks + [m ^ mask for mask in stage for m in masks]
        if k == 1:
            held, early, turned = lax.optimization_barrier((held, early, turned))
    far = swap(held, 1)
    if summed:
        early.append(spans(len(masks) // 2, masks[len(masks) // 2 :], held))
    decays, gates, reach = local
    if summed:
        mine, mate, onehots = pl.pallas_call(
            functools.partial(combine_kernel, masks),
            out_shape=(f32(inner, 2 * width), b16(inner, 2 * width), b16(2, 2 * taps * vocab, span)),
            in_specs=[vmem] * 10,
            out_specs=(vmem,) * 3,
            scratch_shapes=[
                pltpu.VMEM((count, heads, LANES), F32),
                pltpu.VMEM((count, heads, LANES), F32),
                pltpu.VMEM((count, span), jnp.int32),
                pltpu.VMEM((7, count, span), jnp.int32),
                pltpu.VMEM((inner, 2 * width), F32),
            ],
            compiler_params=pltpu.CompilerParams(vmem_limit_bytes=12 * MIB),
            name="combine",
            cost_estimate=pl.CostEstimate(
                flops=1_000_000_000, bytes_accessed=8_000_000, transcendentals=300_000
            ),
        )(held, far, *early[0], *early[1], conv_table, rate_table)
    else:
        masks = masks + [m ^ 1 for m in masks]
        mine, mate, onehots = pl.pallas_call(
            functools.partial(states_kernel, masks),
            out_shape=(
                b16(inner // 2, 2 * width), b16(inner // 2, 2 * width),
                b16(2, 2 * taps * vocab, span),
            ),
            in_specs=[vmem] * 4,
            out_specs=(vmem,) * 3,
            scratch_shapes=[
                pltpu.VMEM((2, count, heads, span), F32),
                pltpu.VMEM((count, heads, span), F32),
                pltpu.VMEM((count, span), jnp.int32),
                pltpu.VMEM((7, count, span), jnp.int32),
                pltpu.VMEM((group, inner // 2, span), BF16),
                pltpu.VMEM((group, 2 * width, span), BF16),
                pltpu.VMEM((inner // 2, 2 * width), F32),
            ],
            compiler_params=pltpu.CompilerParams(vmem_limit_bytes=(20 if count <= 32 else 32) * MIB),
            name="states",
            cost_estimate=pl.CostEstimate(
                flops=10_000_000_000, bytes_accessed=4_000_000, transcendentals=3_000_000
            ),
        )(held, far, conv_table, rate_table)
    mate = swap(mate, 1)
    own = pl.pallas_call(
        own_kernel,
        out_shape=(
            f32(inner, span), b16(inner, span), b16(span, span),
            b16(2, width, span),
        ),
        in_specs=[vmem] * 3,
        out_specs=(vmem,) * 4,
        compiler_params=pltpu.CompilerParams(vmem_limit_bytes=12 * MIB),
        name="own",
        cost_estimate=pl.CostEstimate(
            flops=3_000_000_000, bytes_accessed=9_000_000, transcendentals=1_000_000
        ),
    )(onehots, conv_table, decays)
    return pl.pallas_call(
        functools.partial(output_kernel, summed),
        out_shape=b16(span, inner),
        in_specs=[vmem] * 11,
        out_specs=hbm,
        scratch_shapes=[
            pltpu.VMEM((inner, 2 * width), BF16),
            pltpu.VMEM((2, inner, span), F32),
            pltpu.VMEM((inner, span), BF16),
            pltpu.VMEM((span, inner), BF16),
            pltpu.SemaphoreType.DMA((4,)),
        ],
        compiler_params=pltpu.CompilerParams(vmem_limit_bytes=14 * MIB),
        name="output",
        cost_estimate=pl.CostEstimate(
            flops=2_000_000_000, bytes_accessed=6_000_000, transcendentals=100_000
        ),
    )(
        mine, mate, reach, decays, *own, gates, gain_table, turned,
    )


def solution(mesh):
    in_specs = (
        P(("parts", "seq")),
        P(None, ("parts", "seq")),
        P(), P(), P(), P(), P(), P(), P(), P(),
    )
    out_specs = P(("parts", "seq"), None)
    return jax.shard_map(shards, mesh=mesh, in_specs=in_specs, out_specs=out_specs, check_vma=False)
```
